32 devices in a mesh: group: 4 (over z), fsdp: 4 (over x, core), tensor: 2 (over y).
Axes of the slice: x: 2, y: 2, z: 4, core: 2. Of those that a mesh axis runs over, the one named last changes fastest.
Arguments:
- tokens: bfloat16 [2048, 8192], P(('group', 'fsdp')), may hold values from -6 to 6
- cotangent: bfloat16 [2048, 512], P(('group', 'fsdp'), 'tensor'), may hold values from -0.125 to 0.125
- weight: bfloat16 [8192, 512], P('fsdp', 'tensor'), may hold values from -0.0625 to 0.0625
- moment_one: float32 [8192, 512], P('fsdp', 'tensor'), may hold values from -4 to 4
- moment_two: float32 [8192, 512], P('fsdp', 'tensor'), may hold values from 0.003 to 0.3
- hidden: bfloat16 [4, 512, 8192], P(None, 'group', ('fsdp', 'tensor')), may hold values from -6 to 6
- queries: bfloat16 [4, 512, 4096], P(None, ('group', 'fsdp', 'tensor')), may hold values from -145 to 145
- new_keys: bfloat16 [4, 512, 512], P(None, ('group', 'fsdp', 'tensor')), may hold values from -4 to 4
- key_cache: bfloat16 [512, 32, 512], P(('group', 'fsdp', 'tensor')), may hold values from -4 to 4
- value_cache: bfloat16 [512, 32, 512], P(('group', 'fsdp', 'tensor')), may hold values from -6 to 6
- lengths: int32 [512], P(('group', 'fsdp', 'tensor')), may hold values from 2 to 32
Outputs:
- new_weight: bfloat16 [8192, 512], P('fsdp', 'tensor')
- new_moment_one: float32 [8192, 512], P('fsdp', 'tensor')
- new_moment_two: float32 [8192, 512], P('fsdp', 'tensor')
- attention: bfloat16 [4, 512, 4096], P(None, ('group', 'fsdp', 'tensor'))
The draws below stay inside these ranges and needn't reach their ends.
All inputs are finite; a program needn't handle non-finite values.
Results may differ from the reference program's by a relative error of at most 0.007.
Values may be sent and summed in bfloat16 or wider, within the bound.
A program may use at most 64 MiB of HBM per device.

```python
import math
import jax
import jax.numpy as jnp
from jax import lax

D = 8192
HEAD_DIM = 128
GROUP_HEADS = 8
KV_HEADS = 4
STEPS = 4
ADAM_STEP = 10
ROW_DEV = 16
CACHE = 32
KVW = 512
QW = 4096
TOKENS = 2048
ROWS_ALL = 512
N_GROUP = 4
N_FSDP = 4
N_TENSOR = 2


def joint_draw(key):
    base_key = jax.random.fold_in(key, 7)
    cached = jax.random.normal(jax.random.fold_in(base_key, 1), (ROWS_ALL, CACHE, KV_HEADS, HEAD_DIM), jnp.float32)
    cached = jnp.clip(cached, -4.0, 4.0)
    query_f = jax.random.normal(jax.random.fold_in(base_key, 2), (STEPS, ROWS_ALL, KV_HEADS, GROUP_HEADS, HEAD_DIM), jnp.float32)
    query_f = jnp.clip(query_f, -6.0, 6.0)
    return (cached.reshape(ROWS_ALL, CACHE, KVW), query_f.reshape(STEPS, ROWS_ALL, QW))


def draw_queries(key, part):
    return joint_draw(key)[1].astype(jnp.bfloat16)


def draw_key_cache(key, part):
    return joint_draw(key)[0].astype(jnp.bfloat16)


def touch_ends(entries, stream_key, least, top_value):
    extent = entries.shape
    place = [jax.random.randint(jax.random.fold_in(stream_key, axis), (), 0, extent[axis]) for axis in range(len(extent))]
    entries = entries.at[tuple(place)].set(least)
    longest = extent.index(max(extent))
    place[longest] = (place[longest] + 1) % extent[longest]
    return entries.at[tuple(place)].set(top_value)


def block_levels(rng, extent, cuts, smallest, high):
    def one(axis_at, blocks):
        draws = jax.random.uniform(jax.random.fold_in(jax.random.fold_in(rng, 6), axis_at), (blocks,), jnp.float32, smallest / len(cuts), high / len(cuts))
        return jnp.repeat(jnp.exp(draws), extent[axis_at] // blocks).reshape((-1,) + (1,) * (len(extent) - axis_at - 1))

    loudness = one(*cuts[0])
    for cut in cuts[1:]:
        loudness = loudness * one(*cut)
    return loudness


def centred(own_key, shape, width, limit, shards=(), kind=jnp.bfloat16):
    loudness = block_levels(own_key, shape, shards, -0.22, 0.18) if shards else 1.0
    entries = jax.random.normal(own_key, shape, jnp.float32) * width * loudness
    return jnp.minimum(jnp.maximum(entries, -limit), limit).astype(kind)


def setup_inputs(seed: int = 0) -> dict:
    key_list = jax.random.split(jax.random.key(seed), 12)
    return {
        "tokens": centred(key_list[0], (TOKENS, D), 1.0, 6.0, ((0, 16),)),
        "cotangent": centred(key_list[1], (TOKENS, KVW), TOKENS ** -0.5, 0.125, ((0, 16), (1, 2))),
        "weight": centred(key_list[2], (D, KVW), D ** -0.5, 0.0625, ((0, 4), (1, 2))),
        "moment_one": centred(key_list[3], (D, KVW), 1.0, 4.0, ((0, 4), (1, 2)), jnp.float32),
        "moment_two": jnp.clip(jnp.exp(math.log(0.3) - 4.6051702 * jax.random.uniform(key_list[4], (D, KVW), jnp.float32) ** block_levels(key_list[4], (D, KVW), ((0, 4), (1, 2)), -0.2, 0.2)), 0.003, 0.3),
        "hidden": centred(key_list[5], (STEPS, ROWS_ALL, D), 1.0, 6.0, ((1, 4), (2, 8))),
        "queries": draw_queries(jax.random.fold_in(key_list[11], 71), 0),
        "new_keys": centred(key_list[7], (STEPS, ROWS_ALL, KVW), 1.0, 4.0, ((1, 32),)),
        "key_cache": draw_key_cache(jax.random.fold_in(key_list[11], 71), 0),
        "value_cache": centred(key_list[9], (ROWS_ALL, CACHE, KVW), 1.0, 6.0, ((0, 32),)),
        "lengths": touch_ends(jax.random.randint(key_list[10], (ROWS_ALL,), 2, CACHE + 1), jax.random.fold_in(key_list[10], 1), 2, CACHE).astype(jnp.int32),
    }


learn_rate = 0.001
beta_one = 0.9
beta_two = 0.95
epsilon = 1e-08
decay_rate = 0.1
masked_score = -1e+30

def apply_adamw(gradient, weight, moment_one, moment_two):
    first_new = beta_one * moment_one + (1.0 - beta_one) * gradient
    second_new = beta_two * moment_two + (1.0 - beta_two) * gradient * gradient
    first_hat = first_new / (1.0 - beta_one ** ADAM_STEP)
    second_hat = second_new / (1.0 - beta_two ** ADAM_STEP)
    stepped = weight.astype(jnp.float32) * (1.0 - learn_rate * decay_rate) - learn_rate * first_hat / (jnp.sqrt(second_hat) + epsilon)
    return (stepped.astype(jnp.bfloat16), first_new, second_new)

def attend(queries, new_keys, fresh_values, key_cache, value_cache, lengths):
    row_total = lengths.shape[0]
    query_f = queries.reshape(STEPS, row_total, KV_HEADS, GROUP_HEADS, HEAD_DIM).astype(jnp.float32)
    cached_keys = key_cache.reshape(row_total, CACHE, KV_HEADS, HEAD_DIM).astype(jnp.float32)
    cached_values = value_cache.reshape(row_total, CACHE, KV_HEADS, HEAD_DIM).astype(jnp.float32)
    fresh_keys = new_keys.reshape(STEPS, row_total, KV_HEADS, HEAD_DIM).astype(jnp.float32)
    fresh_vals = fresh_values.reshape(STEPS, row_total, KV_HEADS, HEAD_DIM).astype(jnp.float32)
    score_scale = HEAD_DIM ** (-0.5)
    cached_scores = jnp.einsum('tnhjd,nphd->nhjtp', query_f, cached_keys) * score_scale
    fresh_scores = jnp.einsum('tnhjd,snhd->nhjts', query_f, fresh_keys) * score_scale
    cached_valid = jnp.arange(CACHE, dtype=jnp.int32)[None, :] < lengths[:, None]
    fresh_valid = jnp.arange(STEPS, dtype=jnp.int32)[None, :] <= jnp.arange(STEPS, dtype=jnp.int32)[:, None]
    cached_scores = jnp.where(cached_valid[:, None, None, None, :], cached_scores, masked_score)
    fresh_scores = jnp.where(fresh_valid[None, None, None, :, :], fresh_scores, masked_score)
    highest = jnp.maximum(lax.optimization_barrier(jnp.max(cached_scores, axis=-1)), lax.optimization_barrier(jnp.max(fresh_scores, axis=-1)))[..., None]
    cached_exp = jnp.exp(cached_scores - highest)
    fresh_exp = jnp.exp(fresh_scores - highest)
    denominator = lax.optimization_barrier(jnp.sum(cached_exp, axis=-1, keepdims=True)) + lax.optimization_barrier(jnp.sum(fresh_exp, axis=-1, keepdims=True))
    cached_probs = (cached_exp / denominator).astype(jnp.bfloat16).astype(jnp.float32)
    fresh_probs = (fresh_exp / denominator).astype(jnp.bfloat16).astype(jnp.float32)
    result = jnp.einsum('nhjtp,nphd->tnhjd', cached_probs, cached_values)
    result = result + jnp.einsum('nhjts,snhd->tnhjd', fresh_probs, fresh_vals)
    return result.reshape(STEPS, row_total, QW).astype(jnp.bfloat16)

def block_attend(packed):
    return attend(*packed)

def reference(tokens, cotangent, weight, moment_one, moment_two, hidden, queries, new_keys, key_cache, value_cache, lengths):
    gradient = lax.dot_general(tokens, cotangent, (((0,), (0,)), ((), ())), preferred_element_type=jnp.float32)
    new_weight, first_new, second_new = apply_adamw(gradient, weight, moment_one, moment_two)
    fresh = jnp.stack([jnp.dot(hidden[turn_index], new_weight, preferred_element_type=jnp.float32) for turn_index in range(STEPS)]).astype(jnp.bfloat16)
    group_rows = ROW_DEV * N_FSDP * N_TENSOR
    query_blocks = jnp.moveaxis(queries.reshape(STEPS, N_GROUP, group_rows, QW), 1, 0)
    key_blocks = jnp.moveaxis(new_keys.reshape(STEPS, N_GROUP, group_rows, KVW), 1, 0)
    fresh_blocks = jnp.moveaxis(fresh.reshape(STEPS, N_GROUP, group_rows, KVW), 1, 0)
    cache_keys = key_cache.reshape(N_GROUP, group_rows, CACHE, KVW)
    cache_values = value_cache.reshape(N_GROUP, group_rows, CACHE, KVW)
    length_blocks = lengths.reshape(N_GROUP, group_rows)
    outputs = lax.map(block_attend, (query_blocks, key_blocks, fresh_blocks, cache_keys, cache_values, length_blocks))
    attention = jnp.moveaxis(outputs, 0, 1).reshape(STEPS, ROWS_ALL, QW)
    return (new_weight, first_new, second_new, attention)
```

```python
import functools

import jax
import jax.numpy as jnp
from jax import lax
from jax.experimental import pallas as pl
from jax.experimental.pallas import tpu as pltpu
from jax.sharding import PartitionSpec as P

HEAD_DIM = 128
GROUP_HEADS = 8
KV_HEADS = 4
STEPS = 4
ADAM_STEP = 10

CHUNKS = 8
SPLIT = 2
LAG = 2
CAST_LAG = 3
ATT_PARTS = 8

learn_rate = 0.001
beta_one = 0.9
beta_two = 0.95
epsilon = 1e-08
decay_rate = 0.1
masked_score = -1e30

MESH = pl.DeviceIdType.MESH


def adamw(gradient, weight, moment_one, moment_two):
    first_new = beta_one * moment_one + (1.0 - beta_one) * gradient
    second_new = beta_two * moment_two + (1.0 - beta_two) * gradient * gradient
    first_hat = first_new * (1.0 / (1.0 - beta_one**ADAM_STEP))
    second_hat = second_new * (1.0 / (1.0 - beta_two**ADAM_STEP))
    stepped = weight.astype(jnp.float32) * (
        1.0 - learn_rate * decay_rate
    ) - learn_rate * first_hat / (jnp.sqrt(second_hat) + epsilon)
    return stepped.astype(jnp.bfloat16), first_new, second_new


def kernel(
    n_g, n_f, n_t, n_c,
    lens, tokens, cot, weight, mom1, mom2, hidden, queries, new_keys, kcache, vcache,
    w_v, m1_v, m2_v, att_v,
    tok, cots, hid, own, sb, rf, rb, gt, q_v, nk_v, kc_v, vc_v,
    oc, pf, acc, ps, pr,
    tok_s, tok_r, cot_s, cot_r, hid_s, hid_r, rs_s, agl_s, agr_s, rf_r, rb_r, gt_r,
    pr_s, pr_r, loc, tok_l, hid_l,
):
    g = lax.axis_index("group")
    f = lax.axis_index("fsdp")
    t = lax.axis_index("tensor")
    n_ft = n_f * n_t
    me = f * n_t + t
    rows_c = tok.shape[3]
    rows = n_c * rows_c
    piece = own.shape[2]
    n_s = own.shape[0]
    split = n_s // n_c
    per_t = n_c // n_t
    row_dev = kc_v.shape[0]
    cache = kc_v.shape[1]
    kvw = kc_v.shape[2]
    width = cot.shape[1]

    barrier = pltpu.get_barrier_semaphore()
    for k in range(1, n_ft):
        peer = lax.rem(me + k, n_ft)
        pl.semaphore_signal(
            barrier, inc=1, device_id={"fsdp": peer // n_t, "tensor": peer % n_t}, device_id_type=MESH
        )
    for k in (1, n_g - 1):
        pl.semaphore_signal(
            barrier, inc=1, device_id={"group": lax.rem(g + k, n_g)}, device_id_type=MESH
        )
    def local(src, dst, sem):
        copy = pltpu.make_async_copy(src, dst, sem)
        copy.start()
        return copy

    cot_l = local(cot, cots.at[0], loc.at[0])
    loads_att = [
        local(queries, q_v, loc.at[1]),
        local(new_keys, nk_v, loc.at[2]),
        local(kcache, kc_v, loc.at[3]),
        local(vcache, vc_v, loc.at[4]),
    ]

    def tok_local(c):
        col = pl.multiple_of(f * rows + c * rows_c, rows_c)
        return pltpu.make_async_copy(tokens.at[:, pl.ds(col, rows_c)], tok.at[c, 0], tok_l.at[c])

    for c in range(n_c):
        tok_local(c).start()
    def hid_local(j):
        return pltpu.make_async_copy(
            hidden.at[:, :, pl.ds(j * rows_c, rows_c)], hid.at[t * per_t + j], hid_l.at[j]
        )


    pl.semaphore_wait(barrier, n_ft - 1 + 2)

    def fsdp_peer(k):
        return (f // 2 * 2 + k // 2 * 2) % n_f + (f % 2 + k % 2) % 2

    def cot_copy(k):
        return pltpu.make_async_remote_copy(
            src_ref=cots.at[k - 1] if k % 2 else cot, dst_ref=cots.at[k],
            send_sem=cot_s.at[k], recv_sem=cot_r.at[k],
            device_id={"fsdp": fsdp_peer(1 if k % 2 else k)}, device_id_type=MESH,
        )

    def tok_copy(c, k):
        peer = fsdp_peer(k)
        col = pl.multiple_of(peer * rows + c * rows_c, rows_c)
        return pltpu.make_async_remote_copy(
            src_ref=tokens.at[:, pl.ds(col, rows_c)], dst_ref=tok.at[c, k],
            send_sem=tok_s.at[c, k], recv_sem=tok_r.at[c, k],
            device_id={"fsdp": peer}, device_id_type=MESH,
        )

    def hid_copy(j, k, owner):
        return pltpu.make_async_remote_copy(
            src_ref=hidden.at[:, :, pl.ds(j * rows_c, rows_c)], dst_ref=hid.at[owner * per_t + j],
            send_sem=hid_s.at[j, k], recv_sem=hid_r.at[j, k],
            device_id={"tensor": lax.rem(t + k, n_t)}, device_id_type=MESH,
        )

    for k in range(2, n_f, 2):
        cot_copy(k).start()
    cot_l.wait()
    cot_copy(1).start()
    for c in range(n_c):
        for k in range(1, n_f):
            tok_copy(c, k).start()
    for j in range(per_t):
        for k in range(1, n_t):
            hid_copy(j, k, t).start()

    loads_adam = [
        local(weight, w_v, loc.at[5]),
        local(mom1, m1_v, loc.at[6]),
        local(mom2, m2_v, loc.at[7]),
    ]

    for j in range(per_t):
        hid_local(j).start()
    for k in range(2, n_f, 2):
        cot_copy(k).wait_recv()
        cot_copy(k + 1).start()
    for copy in loads_att:
        copy.wait()
    acc[...] = jnp.zeros_like(acc)

    heads_part = KV_HEADS * GROUP_HEADS // ATT_PARTS

    def attend(part):
        h = part * heads_part // GROUP_HEADS
        qs = [
            q_v[:, :, pl.ds(pl.multiple_of((part * heads_part + j) * HEAD_DIM, HEAD_DIM), HEAD_DIM)]
            .reshape(STEPS * row_dev, HEAD_DIM)
            for j in range(heads_part)
        ]
        q = jnp.concatenate(qs, axis=0)
        cols = pl.ds(pl.multiple_of(h * HEAD_DIM, HEAD_DIM), HEAD_DIM)
        kk = kc_v[:, :, cols].reshape(row_dev * cache, HEAD_DIM)
        fk = nk_v[:, :, cols].reshape(STEPS * row_dev, HEAD_DIM)
        vv = vc_v[:, :, cols].reshape(row_dev * cache, HEAD_DIM)
        contract = (((1,), (1,)), ((), ()))
        scale = HEAD_DIM ** (-0.5)
        s_c = lax.dot_general(q, kk, contract, preferred_element_type=jnp.float32) * scale
        s_f = lax.dot_general(q, fk, contract, preferred_element_type=jnp.float32) * scale
        n_q = q.shape[0]
        col_c = lax.broadcasted_iota(jnp.int32, (1, row_dev * cache), 1)
        col_row = col_c // cache
        limit = jnp.zeros_like(col_c)
        for r in range(row_dev):
            limit = jnp.where(col_row == r, lens[r], limit)
        col_row = jnp.where(col_c % cache < limit, col_row, -1)
        q_id = lax.broadcasted_iota(jnp.int32, (n_q, 1), 0)
        q_row = q_id % row_dev
        q_step = (q_id // row_dev) % STEPS
        col_f = lax.broadcasted_iota(jnp.int32, (1, STEPS * row_dev), 1)
        ok_c = q_row == col_row
        ok_f = (q_row == col_f % row_dev) & (col_f // row_dev <= q_step)
        s_c = jnp.where(ok_c, s_c, masked_score)
        s_f = jnp.where(ok_f, s_f, masked_score)
        highest = jnp.maximum(
            jnp.max(s_c, axis=-1, keepdims=True), jnp.max(s_f, axis=-1, keepdims=True)
        )
        e_c = jnp.exp(s_c - highest)
        e_f = jnp.exp(s_f - highest)
        den = jnp.sum(e_c, axis=-1, keepdims=True) + jnp.sum(e_f, axis=-1, keepdims=True)
        p_c = (e_c / den).astype(jnp.bfloat16)
        pf[part] = (e_f / den).astype(jnp.bfloat16)
        oc[part] = jnp.dot(p_c, vv, preferred_element_type=jnp.float32)

    owners = ((n_g - 1) // 2, n_g // 2)
    final = n_g // 2

    def chain(c, p, buf_src, buf_dst, send, recv, to):
        return pltpu.make_async_remote_copy(
            src_ref=buf_src.at[c, p], dst_ref=buf_dst.at[c, p],
            send_sem=send.at[c, p], recv_sem=recv.at[c, p],
            device_id={"group": lax.rem(g + to + n_g, n_g)}, device_id_type=MESH,
        )

    def rs_right(c, p):
        return chain(c, p, sb, rf, rs_s, rf_r, 1)

    def rs_left(c, p):
        return chain(c, p, sb, rb, rs_s, rb_r, -1)

    def ag_right(c, p):
        return chain(c, p, gt, gt, agr_s, gt_r, 1)

    def ag_left(c, p):
        return chain(c, p, gt, gt, agl_s, gt_r, -1)

    def active(c):
        return (c >= 0) & (c < n_s)


    for k in range(1, n_f, 2):
        cot_copy(k).wait_recv()

    def slot(s, carry):
        @pl.when((s < n_s) & (s % split == 0))
        def _():
            b = s // split
            tok_local(b).wait()
            for k in range(1, n_f):
                tok_copy(b, k).wait_recv()
            block = tok[b].reshape(n_f * tok.shape[2], rows_c)
            grad = lax.dot_general(
                block, cots[...].reshape(n_f * tok.shape[2], width), (((0,), (0,)), ((), ())),
                preferred_element_type=jnp.float32,
            )
            for u in range(split):
                for p in range(2):
                    at = (2 * u + p) * piece
                    own[s + u, p] = grad[at : at + piece]

        for p in range(2):
            o = owners[p]
            if o > 0:
                c = s - LAG * g

                @pl.when((g < o) & active(c))
                def _():
                    @pl.when(g == 0)
                    def _():
                        sb[c, p] = own[c, p].astype(jnp.bfloat16)

                    @pl.when(g > 0)
                    def _():
                        rs_right(c, p).wait_recv()
                        sb[c, p] = (own[c, p] + rf[c, p].astype(jnp.float32)).astype(jnp.bfloat16)

                    rs_right(c, p).start()

            if o < n_g - 1:
                c2 = s - LAG * (n_g - 1 - g)

                @pl.when((g > o) & active(c2))
                def _():
                    @pl.when(g == n_g - 1)
                    def _():
                        sb[c2, p] = own[c2, p].astype(jnp.bfloat16)

                    @pl.when(g < n_g - 1)
                    def _():
                        rs_left(c2, p).wait_recv()
                        sb[c2, p] = (own[c2, p] + rb[c2, p].astype(jnp.float32)).astype(
                            jnp.bfloat16
                        )

                    rs_left(c2, p).start()

        for p in range(2):
            o = owners[p]
            c3 = s - LAG * final

            @pl.when((g == o) & active(c3))
            def _():
                total = own[c3, p]
                if o > 0:
                    rs_right(c3, p).wait_recv()
                    total = total + rf[c3, p].astype(jnp.float32)
                if o < n_g - 1:
                    rs_left(c3, p).wait_recv()
                    total = total + rb[c3, p].astype(jnp.float32)
                gt[c3, p] = total.astype(jnp.bfloat16)
                if o > 0:
                    ag_left(c3, p).start()
                if o < n_g - 1:
                    ag_right(c3, p).start()

            c4 = s - LAG * final - CAST_LAG * jnp.abs(g - o)

            @pl.when((g > o) & active(c4))
            def _():
                ag_right(c4, p).wait_recv()

                @pl.when(g < n_g - 1)
                def _():
                    ag_right(c4, p).start()

            @pl.when((g < o) & active(c4))
            def _():
                ag_left(c4, p).wait_recv()

                @pl.when(g > 0)
                def _():
                    ag_left(c4, p).start()

        @pl.when(s == LAG * final)
        def _():
            for copy in loads_adam:
                copy.wait()
            for j in range(per_t):
                hid_local(j).wait()

        far = jnp.maximum(jnp.abs(g - owners[0]), jnp.abs(g - owners[1]))
        last = s - LAG * final - CAST_LAG * far

        @pl.when(active(last) & (last % split == split - 1))
        def _():
            b = last // split
            for k in range(1, n_t):
                owner = lax.rem(t + n_t - k, n_t)

                @pl.when(b // per_t == owner)
                def _():
                    hid_copy(lax.rem(b, per_t), k, owner).wait_recv()

            span = pl.ds(pl.multiple_of(b * rows_c, rows_c), rows_c)
            grad = gt[pl.ds(b * split, split)].reshape(rows_c, width).astype(jnp.float32)
            w_new, m1_new, m2_new = adamw(grad, w_v[span], m1_v[span], m2_v[span])
            w_v[span] = w_new
            m1_v[span] = m1_new
            m2_v[span] = m2_new
            lhs = hid[b].reshape(acc.shape[0], rows_c)
            acc[...] += jnp.dot(lhs, w_new, preferred_element_type=jnp.float32)

        @pl.when((s % split == split - 1) & (s < split * ATT_PARTS))
        def _():
            attend(s // split)

        return carry

    reach = max(owners[1], n_g - 1 - owners[0])
    lax.fori_loop(0, max(n_s + LAG * final + CAST_LAG * reach, split * ATT_PARTS), slot, 0)

    def out_copy(k):
        peer = lax.rem(me + k, n_ft)
        return pltpu.make_async_remote_copy(
            src_ref=ps.at[k], dst_ref=pr.at[t, f], send_sem=pr_s.at[k], recv_sem=pr_r.at[k],
            device_id={"fsdp": peer // n_t, "tensor": peer % n_t}, device_id_type=MESH,
        )

    ps_all = acc.reshape(STEPS, acc.shape[0] // STEPS, width)
    for k in range(1, n_ft):
        peer = lax.rem(me + k, n_ft)
        take = pl.ds(pl.multiple_of(peer * row_dev, row_dev), row_dev)
        ps[k] = ps_all[:, take, :].reshape(STEPS * row_dev, width).astype(jnp.bfloat16)
        out_copy(k).start()
    take = pl.ds(pl.multiple_of(me * row_dev, row_dev), row_dev)
    pr[t, f] = ps_all[:, take, :].reshape(STEPS * row_dev, width).astype(jnp.bfloat16)
    for k in range(1, n_ft):
        src = lax.rem(me + n_ft - k, n_ft)
        pltpu.make_async_remote_copy(
            src_ref=ps.at[k], dst_ref=pr.at[src % n_t, src // n_t],
            send_sem=pr_s.at[k], recv_sem=pr_r.at[k],
            device_id={"fsdp": f}, device_id_type=MESH,
        ).wait_recv()
    fresh_parts = []
    for tt in range(n_t):
        total = pr[tt, 0].astype(jnp.float32)
        for ff in range(1, n_f):
            total = total + pr[tt, ff].astype(jnp.float32)
        fresh_parts.append(total.astype(jnp.bfloat16))
    fresh = jnp.concatenate(fresh_parts, axis=1)
    block = STEPS * row_dev
    for part in range(ATT_PARTS):
        h = part * heads_part // GROUP_HEADS
        res = oc[part] + jnp.dot(
            pf[part], fresh[:, h * HEAD_DIM : (h + 1) * HEAD_DIM], preferred_element_type=jnp.float32
        )
        for j in range(heads_part):
            at = (part * heads_part + j) * HEAD_DIM
            att_v[:, :, at : at + HEAD_DIM] = (
                res[j * block : (j + 1) * block].reshape(STEPS, row_dev, HEAD_DIM).astype(jnp.bfloat16)
            )

    for k in range(1, n_f):
        cot_copy(k).wait_send()
        for c in range(n_c):
            tok_copy(c, k).wait_send()
    for k in range(1, n_t):
        for j in range(per_t):
            hid_copy(j, k, t).wait_send()
    for k in range(1, n_ft):
        out_copy(k).wait_send()

    def drain(c, carry):
        for p in range(2):
            o = owners[p]

            @pl.when(g != o)
            def _():
                rs_right(c, p).wait_send()

            @pl.when((g >= o) & (g < n_g - 1))
            def _():
                ag_right(c, p).wait_send()

            @pl.when((g <= o) & (g > 0))
            def _():
                ag_left(c, p).wait_send()

        return carry

    lax.fori_loop(0, n_s, drain, 0)


def store_kernel(w_v, m1_v, m2_v, att_v, w_o, m1_o, m2_o, att_o, sems):
    copies = []
    n = 0
    for a, o, k in ((m1_v, m1_o, 4), (m2_v, m2_o, 4), (w_v, w_o, 2)):
        rows = a.shape[0] // k
        for j in range(k):
            span = pl.ds(j * rows, rows)
            copies.append(pltpu.make_async_copy(a.at[span], o.at[span], sems.at[n]))
            n += 1
    copies.append(pltpu.make_async_copy(att_v, att_o, sems.at[n]))
    for c in copies:
        c.start()
    for c in copies:
        c.wait()


def store(*arrays):
    spec = pl.BlockSpec(memory_space=pl.ANY)
    return pl.pallas_call(
        store_kernel,
        out_shape=tuple(jax.ShapeDtypeStruct(a.shape, a.dtype) for a in arrays),
        in_specs=[pl.BlockSpec(memory_space=pltpu.VMEM)] * 4, out_specs=(spec,) * 4,
        scratch_shapes=[pltpu.SemaphoreType.DMA((11,))],
        compiler_params=pltpu.CompilerParams(vmem_limit_bytes=16 * 1024 * 1024),
        name="store",
    )(*[pltpu.with_memory_space_constraint(a, pltpu.VMEM) for a in arrays])


def per_device(
    n_g, n_f, n_t,
    tokens, cotangent, weight, moment_one, moment_two, hidden, queries, new_keys,
    key_cache, value_cache, lengths,
):
    n_ft = n_f * n_t
    rows, width = weight.shape
    n_c = max(CHUNKS, n_t)
    rows_c = rows // n_c
    row_dev, cache, kvw = key_cache.shape
    tok_rows = tokens.shape[0]
    n_s = n_c * SPLIT
    piece_shape = (n_s, 2, rows // n_s // 2, width)
    acc_rows = hidden.shape[0] * hidden.shape[1]
    n_q = KV_HEADS * GROUP_HEADS // ATT_PARTS * STEPS * row_dev
    bf16, f32 = jnp.bfloat16, jnp.float32
    dma = pltpu.SemaphoreType.DMA
    anywhere = pl.BlockSpec(memory_space=pl.ANY)
    scratch = [
        pltpu.VMEM((n_c, n_f, tok_rows, rows_c), bf16),
        pltpu.VMEM((n_f, tok_rows, width), bf16),
        pltpu.VMEM((n_c,) + hidden.shape[:2] + (rows_c,), bf16),
        pltpu.VMEM(piece_shape, f32),
        pltpu.VMEM(piece_shape, bf16),
        pltpu.VMEM(piece_shape, bf16),
        pltpu.VMEM(piece_shape, bf16),
        pltpu.VMEM(piece_shape, bf16),
        pltpu.VMEM(queries.shape, bf16),
        pltpu.VMEM(new_keys.shape, bf16),
        pltpu.VMEM(key_cache.shape, bf16),
        pltpu.VMEM(value_cache.shape, bf16),
        pltpu.VMEM((ATT_PARTS, n_q, HEAD_DIM), f32),
        pltpu.VMEM((ATT_PARTS, n_q, STEPS * row_dev), bf16),
        pltpu.VMEM((acc_rows, width), f32),
        pltpu.VMEM((n_ft, STEPS * row_dev, width), bf16),
        pltpu.VMEM((n_t, n_f, STEPS * row_dev, width), bf16),
        dma((n_c, n_f)), dma((n_c, n_f)),
        dma((n_f,)), dma((n_f,)),
        dma((n_c // n_t, n_t)), dma((n_c // n_t, n_t)),
        dma((n_s, 2)), dma((n_s, 2)), dma((n_s, 2)),
        dma((n_s, 2)), dma((n_s, 2)), dma((n_s, 2)),
        dma((n_ft,)), dma((n_ft,)),
        dma((9,)), dma((n_c,)), dma((n_c // n_t,)),
    ]
    return store(*pl.pallas_call(
        functools.partial(kernel, n_g, n_f, n_t, n_c),
        out_shape=(
            pltpu.VMEM(weight.shape, bf16),
            pltpu.VMEM(weight.shape, f32),
            pltpu.VMEM(weight.shape, f32),
            pltpu.VMEM(queries.shape, bf16),
        ),
        in_specs=[pl.BlockSpec(memory_space=pltpu.SMEM)] + [anywhere] * 10,
        out_specs=(pl.BlockSpec(memory_space=pltpu.VMEM),) * 4,
        scratch_shapes=scratch,
        compiler_params=pltpu.CompilerParams(
            collective_id=0, has_side_effects=True, vmem_limit_bytes=50 * 1024 * 1024
        ),
        name="step",
    )(
        lengths, tokens, cotangent, weight, moment_one, moment_two, hidden, queries, new_keys,
        key_cache, value_cache,
    ))


def solution(mesh):
    in_specs = (
        P(("group", "fsdp"), None),
        P(("group", "fsdp"), "tensor"),
        P("fsdp", "tensor"),
        P("fsdp", "tensor"),
        P("fsdp", "tensor"),
        P(None, "group", ("fsdp", "tensor")),
        P(None, ("group", "fsdp", "tensor"), None),
        P(None, ("group", "fsdp", "tensor"), None),
        P(("group", "fsdp", "tensor"), None, None),
        P(("group", "fsdp", "tensor"), None, None),
        P(("group", "fsdp", "tensor")),
    )
    out_specs = (
        P("fsdp", "tensor"),
        P("fsdp", "tensor"),
        P("fsdp", "tensor"),
        P(None, ("group", "fsdp", "tensor"), None),
    )
    sizes = (mesh.shape["group"], mesh.shape["fsdp"], mesh.shape["tensor"])
    return jax.shard_map(
        functools.partial(per_device, *sizes),
        mesh=mesh, in_specs=in_specs, out_specs=out_specs, check_vma=False,
    )
```

```python
import functools

import jax
import jax.numpy as jnp
from jax import lax
from jax.experimental import pallas as pl
from jax.experimental.pallas import tpu as pltpu
from jax.sharding import PartitionSpec as P

HEAD_DIM = 128
GROUP_HEADS = 8
KV_HEADS = 4
STEPS = 4
ADAM_STEP = 10

CHUNKS = 16
PIECES = 2
IN_LAG = 2
MID_LAG = 3
OUT_LAG = 3
ATT_PARTS = 8
ATT_FIRST = 4
AHEAD = 3

learn_rate = 0.001
beta_one = 0.9
beta_two = 0.95
epsilon = 1e-08
decay_rate = 0.1
masked_score = -1e30

MESH = pl.DeviceIdType.MESH


def adamw(gradient, weight, moment_one, moment_two):
    first_new = beta_one * moment_one + (1.0 - beta_one) * gradient
    second_new = beta_two * moment_two + (1.0 - beta_two) * gradient * gradient
    first_hat = first_new * (1.0 / (1.0 - beta_one**ADAM_STEP))
    second_hat = second_new * (1.0 / (1.0 - beta_two**ADAM_STEP))
    stepped = weight.astype(jnp.float32) * (
        1.0 - learn_rate * decay_rate
    ) - learn_rate * first_hat / (jnp.sqrt(second_hat) + epsilon)
    return stepped.astype(jnp.bfloat16), first_new, second_new


def kernel(
    n_g, n_f, n_t, n_c,
    lens, tokens, cot, weight, mom1, mom2, hidden, queries, new_keys, kcache, vcache,
    w_v, m1_v, m2_v, oc, pf, fresh,
    tok, cots, hid, own, sb, r1, r2, gt, q_v, nk_v, kc_v, vc_v,
    acc, ps, pr,
    tok_s, tok_r, cot_s, cot_r, hid_s, hid_r, in_s, out_s, r1_r, r2_r, gt_r,
    pr_s, pr_r, loc, tok_l, hid_l,
):
    g = lax.axis_index("group")
    f = lax.axis_index("fsdp")
    t = lax.axis_index("tensor")
    n_ft = n_f * n_t
    me = f * n_t + t
    rows_c = tok.shape[3]
    rows = n_c * rows_c
    per_t = n_c // n_t
    row_dev = kc_v.shape[0]
    cache = kc_v.shape[1]
    width = cot.shape[1]

    mid_l, mid_r = n_g // 2 - 1, n_g // 2
    on_left = g <= mid_l
    toward = jnp.where(on_left, 1, -1)
    depth = jnp.where(on_left, g, n_g - 1 - g)
    mid_depth = jnp.where(on_left, mid_l, n_g - 1 - mid_r)
    is_mid = depth == mid_depth
    max_depth = max(mid_l, n_g - 1 - mid_r)

    barrier = pltpu.get_barrier_semaphore()
    for k in range(1, n_ft):
        peer = lax.rem(me + k, n_ft)
        pl.semaphore_signal(
            barrier, inc=1, device_id={"fsdp": peer // n_t, "tensor": peer % n_t}, device_id_type=MESH
        )

    def tell(to):
        pl.semaphore_signal(
            barrier, inc=1, device_id={"group": lax.rem(g + to + n_g, n_g)}, device_id_type=MESH
        )

    @pl.when(is_mid)
    def _():
        tell(toward)

    def local(src, dst, sem):
        copy = pltpu.make_async_copy(src, dst, sem)
        copy.start()
        return copy

    def row_block(c):
        return lax.rem(c + t * per_t, n_c)

    def tok_local(c):
        col = pl.multiple_of(f * rows + row_block(c) * rows_c, rows_c)
        return pltpu.make_async_copy(tokens.at[:, pl.ds(col, rows_c)], tok.at[c, 0], tok_l.at[c])

    def hid_local(j):
        return pltpu.make_async_copy(
            hidden.at[:, :, pl.ds(j * rows_c, rows_c)], hid.at[t * per_t + j], hid_l.at[j]
        )

    cot_l = local(cot, cots.at[0], loc.at[0])
    loads_att = [
        local(queries, q_v, loc.at[1]),
        local(new_keys, nk_v, loc.at[2]),
        local(kcache, kc_v, loc.at[3]),
        local(vcache, vc_v, loc.at[4]),
    ]
    for c in range(AHEAD):
        tok_local(c).start()

    @pl.when((depth == 0) & jnp.logical_not(is_mid))
    def _():
        pl.semaphore_wait(barrier, n_ft - 1)

    @pl.when((depth == 0) & is_mid)
    def _():
        pl.semaphore_wait(barrier, n_ft)

    @pl.when((depth > 0) & jnp.logical_not(is_mid))
    def _():
        pl.semaphore_wait(barrier, n_ft)
        tell(-toward)

    @pl.when((depth > 0) & is_mid)
    def _():
        pl.semaphore_wait(barrier, n_ft + 1)
        tell(-toward)

    @pl.when(jnp.logical_not(is_mid))
    def _():
        tell(toward)

    def fsdp_peer(k):
        return (f // 2 * 2 + k // 2 * 2) % n_f + (f % 2 + k % 2) % 2

    def cot_copy(k):
        return pltpu.make_async_remote_copy(
            src_ref=cots.at[k - 1] if k % 2 else cot, dst_ref=cots.at[k],
            send_sem=cot_s.at[k], recv_sem=cot_r.at[k],
            device_id={"fsdp": fsdp_peer(1 if k % 2 else k)}, device_id_type=MESH,
        )

    def tok_copy(c, k):
        peer = fsdp_peer(k)
        col = pl.multiple_of(peer * rows + row_block(c) * rows_c, rows_c)
        return pltpu.make_async_remote_copy(
            src_ref=tokens.at[:, pl.ds(col, rows_c)], dst_ref=tok.at[c, k],
            send_sem=tok_s.at[c, k], recv_sem=tok_r.at[c, k],
            device_id={"fsdp": peer}, device_id_type=MESH,
        )

    def hid_copy(j, k, owner):
        return pltpu.make_async_remote_copy(
            src_ref=hidden.at[:, :, pl.ds(j * rows_c, rows_c)], dst_ref=hid.at[owner * per_t + j],
            send_sem=hid_s.at[j, k], recv_sem=hid_r.at[j, k],
            device_id={"tensor": lax.rem(t + k, n_t)}, device_id_type=MESH,
        )

    def send_tokens(c):
        for k in range(n_f - 1, 0, -1):
            tok_copy(c, k).start()

    for k in range(2, n_f, 2):
        cot_copy(k).start()
    cot_l.wait()
    cot_copy(1).start()
    for c in range(AHEAD):
        send_tokens(c)

    loads_adam = [
        local(weight, w_v, loc.at[5]),
        local(mom1, m1_v, loc.at[6]),
        local(mom2, m2_v, loc.at[7]),
    ]
    for copy in loads_att:
        copy.wait()

    heads_part = KV_HEADS * GROUP_HEADS // ATT_PARTS

    def attend(part):
        h = part * heads_part // GROUP_HEADS
        qs = [
            q_v[:, :, pl.ds(pl.multiple_of((part * heads_part + j) * HEAD_DIM, HEAD_DIM), HEAD_DIM)]
            .reshape(STEPS * row_dev, HEAD_DIM)
            for j in range(heads_part)
        ]
        q = jnp.concatenate(qs, axis=0)
        cols = pl.ds(pl.multiple_of(h * HEAD_DIM, HEAD_DIM), HEAD_DIM)
        kk = kc_v[:, :, cols].reshape(row_dev * cache, HEAD_DIM)
        fk = nk_v[:, :, cols].reshape(STEPS * row_dev, HEAD_DIM)
        vv = vc_v[:, :, cols].reshape(row_dev * cache, HEAD_DIM)
        contract = (((1,), (1,)), ((), ()))
        scale = HEAD_DIM ** (-0.5)
        s_c = lax.dot_general(q, kk, contract, preferred_element_type=jnp.float32) * scale
        s_f = lax.dot_general(q, fk, contract, preferred_element_type=jnp.float32) * scale
        n_q = q.shape[0]
        col_c = lax.broadcasted_iota(jnp.int32, (1, row_dev * cache), 1)
        col_row = col_c // cache
        limit = jnp.zeros_like(col_c)
        for r in range(row_dev):
            limit = jnp.where(col_row == r, lens[r], limit)
        col_row = jnp.where(col_c % cache < limit, col_row, -1)
        q_id = lax.broadcasted_iota(jnp.int32, (n_q, 1), 0)
        q_row = q_id % row_dev
        q_step = (q_id // row_dev) % STEPS
        col_f = lax.broadcasted_iota(jnp.int32, (1, STEPS * row_dev), 1)
        ok_c = q_row == col_row
        ok_f = (q_row == col_f % row_dev) & (col_f // row_dev <= q_step)
        s_c = jnp.where(ok_c, s_c, masked_score)
        s_f = jnp.where(ok_f, s_f, masked_score)
        highest = jnp.maximum(
            jnp.max(s_c, axis=-1, keepdims=True), jnp.max(s_f, axis=-1, keepdims=True)
        )
        e_c = jnp.exp(s_c - highest)
        e_f = jnp.exp(s_f - highest)
        den = jnp.sum(e_c, axis=-1, keepdims=True) + jnp.sum(e_f, axis=-1, keepdims=True)
        p_c = (e_c / den).astype(jnp.bfloat16)
        pf[part] = (e_f / den).astype(jnp.bfloat16)
        oc[part] = jnp.dot(p_c, vv, preferred_element_type=jnp.float32)

    for part in range(ATT_FIRST // 2):
        attend(part)
    for k in range(2, n_f, 2):
        cot_copy(k).wait_recv()
        cot_copy(k + 1).start()
    for part in range(ATT_FIRST // 2, ATT_FIRST):
        attend(part)
    acc[...] = jnp.zeros_like(acc)
    for k in range(1, n_f, 2):
        cot_copy(k).wait_recv()

    @pl.when(jnp.logical_not(is_mid))
    def _():
        pl.semaphore_wait(barrier, 1)

    def inward(c, p, dst, recv):
        return pltpu.make_async_remote_copy(
            src_ref=sb.at[c, p], dst_ref=dst.at[c, p], send_sem=in_s.at[c, p], recv_sem=recv.at[c, p],
            device_id={"group": lax.rem(g + toward + n_g, n_g)}, device_id_type=MESH,
        )

    def outward(c, p):
        return pltpu.make_async_remote_copy(
            src_ref=gt.at[c, p], dst_ref=gt.at[c, p], send_sem=out_s.at[c, p], recv_sem=gt_r.at[c, p],
            device_id={"group": lax.rem(g - toward + n_g, n_g)}, device_id_type=MESH,
        )

    def send_inward(c, p, part):
        sb[c, p] = part.astype(jnp.bfloat16)

        @pl.when(is_mid)
        def _():
            inward(c, p, r2, r2_r).start()

        @pl.when(jnp.logical_not(is_mid))
        def _():
            inward(c, p, r1, r1_r).start()

    def active(c):
        return (c >= 0) & (c < n_c)

    pieces, piece = sb.shape[1:3]
    first_total = IN_LAG * max_depth + MID_LAG

    def slot(s, carry):
        @pl.when(s < n_c - AHEAD)
        def _():
            tok_local(s + AHEAD).start()
            send_tokens(s + AHEAD)

        @pl.when(s < per_t)
        def _():
            for k in range(1, n_t):
                hid_copy(s, k, t).start()
            hid_local(s).start()

        @pl.when(s < n_c)
        def _():
            tok_local(s).wait()
            for k in range(1, n_f):
                tok_copy(s, k).wait_recv()
            grad = lax.dot_general(
                tok[s].reshape(n_f * tok.shape[2], rows_c),
                cots[...].reshape(n_f * tok.shape[2], width), (((0,), (0,)), ((), ())),
                preferred_element_type=jnp.float32,
            )

            @pl.when(depth == 0)
            def _():
                for p in range(pieces):
                    send_inward(s, p, grad[p * piece : (p + 1) * piece])

            @pl.when(depth > 0)
            def _():
                for p in range(pieces):
                    own[s, p] = grad[p * piece : (p + 1) * piece]

        c1 = s - IN_LAG * depth

        @pl.when((depth > 0) & active(c1))
        def _():
            for p in range(pieces):
                inward(c1, p, r1, r1_r).wait_recv()
                send_inward(c1, p, own[c1, p] + r1[c1, p].astype(jnp.float32))

        @pl.when(s == first_total)
        def _():
            for copy in loads_adam:
                copy.wait()

        c2 = s - first_total - OUT_LAG * (mid_depth - depth)

        @pl.when(active(c2))
        def _():
            @pl.when(is_mid)
            def _():
                for p in range(pieces):
                    inward(c2, p, r2, r2_r).wait_recv()
                    total = sb[c2, p].astype(jnp.float32) + r2[c2, p].astype(jnp.float32)
                    gt[c2, p] = total.astype(jnp.bfloat16)

                    @pl.when(depth > 0)
                    def _():
                        outward(c2, p).start()

            @pl.when(jnp.logical_not(is_mid))
            def _():
                for p in range(pieces):
                    outward(c2, p).wait_recv()

                    @pl.when(depth > 0)
                    def _():
                        outward(c2, p).start()

            b = row_block(c2)

            @pl.when(b // per_t == t)
            def _():
                hid_local(lax.rem(b, per_t)).wait()

            for k in range(1, n_t):
                owner = lax.rem(t + n_t - k, n_t)

                @pl.when(b // per_t == owner)
                def _():
                    hid_copy(lax.rem(b, per_t), k, owner).wait_recv()

            span = pl.ds(pl.multiple_of(b * rows_c, rows_c), rows_c)
            w_new, m1_new, m2_new = adamw(
                gt[c2].reshape(rows_c, width).astype(jnp.float32), w_v[span], m1_v[span], m2_v[span]
            )
            w_v[span] = w_new
            m1_v[span] = m1_new
            m2_v[span] = m2_new
            lhs = hid[b].reshape(acc.shape[0], rows_c)
            acc[...] += jnp.dot(lhs, w_new, preferred_element_type=jnp.float32)

        @pl.when(s < ATT_PARTS - ATT_FIRST)
        def _():
            attend(s + ATT_FIRST)

        return carry

    slots = n_c + first_total + OUT_LAG * max_depth
    lax.fori_loop(0, max(slots, ATT_PARTS - ATT_FIRST), slot, 0)

    def out_copy(k):
        peer = lax.rem(me + k, n_ft)
        return pltpu.make_async_remote_copy(
            src_ref=ps.at[k], dst_ref=pr.at[t, f], send_sem=pr_s.at[k], recv_sem=pr_r.at[k],
            device_id={"fsdp": peer // n_t, "tensor": peer % n_t}, device_id_type=MESH,
        )

    ps_all = acc.reshape(STEPS, acc.shape[0] // STEPS, width)
    for k in range(1, n_ft):
        peer = lax.rem(me + k, n_ft)
        take = pl.ds(pl.multiple_of(peer * row_dev, row_dev), row_dev)
        ps[k] = ps_all[:, take, :].reshape(STEPS * row_dev, width).astype(jnp.bfloat16)
        out_copy(k).start()
    take = pl.ds(pl.multiple_of(me * row_dev, row_dev), row_dev)
    pr[t, f] = ps_all[:, take, :].reshape(STEPS * row_dev, width).astype(jnp.bfloat16)
    for k in range(1, n_f):
        cot_copy(k).wait_send()

    def drain(c, carry):
        for k in range(1, n_f):
            tok_copy(c, k).wait_send()
        for p in range(pieces):
            inward(c, p, r1, r1_r).wait_send()

        @pl.when(depth > 0)
        def _():
            for p in range(pieces):
                outward(c, p).wait_send()

        @pl.when(c < per_t)
        def _():
            for k in range(1, n_t):
                hid_copy(c, k, t).wait_send()

        return carry

    lax.fori_loop(0, n_c, drain, 0)
    for k in range(1, n_ft):
        src = lax.rem(me + n_ft - k, n_ft)
        pltpu.make_async_remote_copy(
            src_ref=ps.at[k], dst_ref=pr.at[src % n_t, src // n_t],
            send_sem=pr_s.at[k], recv_sem=pr_r.at[k],
            device_id={"fsdp": f}, device_id_type=MESH,
        ).wait_recv()
    fresh_parts = []
    for tt in range(n_t):
        total = pr[tt, 0].astype(jnp.float32)
        for ff in range(1, n_f):
            total = total + pr[tt, ff].astype(jnp.float32)
        fresh_parts.append(total.astype(jnp.bfloat16))
    fresh[...] = jnp.concatenate(fresh_parts, axis=1)

    for k in range(1, n_ft):
        out_copy(k).wait_send()


def finish_kernel(w_v, m1_v, m2_v, oc, pf, fresh, w_o, m1_o, m2_o, att_o, att_v, sems):
    copies = []
    for a, o, cuts in ((m1_v, m1_o, 4), (m2_v, m2_o, 4), (w_v, w_o, 2)):
        rows = a.shape[0] // cuts
        for j in range(cuts):
            span = pl.ds(j * rows, rows)
            copies.append(pltpu.make_async_copy(a.at[span], o.at[span], sems.at[len(copies)]))
            copies[-1].start()
    heads_part = KV_HEADS * GROUP_HEADS // ATT_PARTS
    steps, row_dev = att_v.shape[:2]
    block = steps * row_dev
    for part in range(ATT_PARTS):
        h = part * heads_part // GROUP_HEADS
        res = oc[part] + jnp.dot(
            pf[part], fresh[:, h * HEAD_DIM : (h + 1) * HEAD_DIM], preferred_element_type=jnp.float32
        )
        for j in range(heads_part):
            at = (part * heads_part + j) * HEAD_DIM
            att_v[:, :, at : at + HEAD_DIM] = (
                res[j * block : (j + 1) * block].reshape(steps, row_dev, HEAD_DIM).astype(jnp.bfloat16)
            )
        cols = pl.ds(part * heads_part * HEAD_DIM, heads_part * HEAD_DIM)
        copies.append(
            pltpu.make_async_copy(att_v.at[:, :, cols], att_o.at[:, :, cols], sems.at[len(copies)])
        )
        copies[-1].start()
    for copy in copies:
        copy.wait()


def finish(att_shape, w, m1, m2, *rest):
    spec = pl.BlockSpec(memory_space=pl.ANY)
    outs = [jax.ShapeDtypeStruct(a.shape, a.dtype) for a in (w, m1, m2)]
    outs.append(jax.ShapeDtypeStruct(att_shape, jnp.bfloat16))
    held = [pltpu.with_memory_space_constraint(a, pltpu.VMEM) for a in (w, m1, m2) + rest]
    return pl.pallas_call(
        finish_kernel,
        out_shape=tuple(outs),
        in_specs=[pl.BlockSpec(memory_space=pltpu.VMEM)] * len(held),
        out_specs=(spec,) * 4,
        scratch_shapes=[pltpu.VMEM(att_shape, jnp.bfloat16), pltpu.SemaphoreType.DMA((10 + ATT_PARTS,))],
        compiler_params=pltpu.CompilerParams(vmem_limit_bytes=16 * 1024 * 1024),
        name="finish",
    )(*held)


def per_device(
    n_g, n_f, n_t,
    tokens, cotangent, weight, moment_one, moment_two, hidden, queries, new_keys,
    key_cache, value_cache, lengths,
):
    n_ft = n_f * n_t
    rows, width = weight.shape
    n_c = max(CHUNKS, n_t)
    rows_c = rows // n_c
    row_dev, cache, kvw = key_cache.shape
    tok_rows = tokens.shape[0]
    piece_shape = (n_c, PIECES, rows_c // PIECES, width)
    acc_rows = hidden.shape[0] * hidden.shape[1]
    n_q = KV_HEADS * GROUP_HEADS // ATT_PARTS * STEPS * row_dev
    bf16, f32 = jnp.bfloat16, jnp.float32
    dma = pltpu.SemaphoreType.DMA
    anywhere = pl.BlockSpec(memory_space=pl.ANY)
    scratch = [
        pltpu.VMEM((n_c, n_f, tok_rows, rows_c), bf16),
        pltpu.VMEM((n_f, tok_rows, width), bf16),
        pltpu.VMEM((n_c,) + hidden.shape[:2] + (rows_c,), bf16),
        pltpu.VMEM(piece_shape, f32),
        pltpu.VMEM(piece_shape, bf16),
        pltpu.VMEM(piece_shape, bf16),
        pltpu.VMEM(piece_shape, bf16),
        pltpu.VMEM(piece_shape, bf16),
        pltpu.VMEM(queries.shape, bf16),
        pltpu.VMEM(new_keys.shape, bf16),
        pltpu.VMEM(key_cache.shape, bf16),
        pltpu.VMEM(value_cache.shape, bf16),
        pltpu.VMEM((acc_rows, width), f32),
        pltpu.VMEM((n_ft, STEPS * row_dev, width), bf16),
        pltpu.VMEM((n_t, n_f, STEPS * row_dev, width), bf16),
        dma((n_c, n_f)), dma((n_c, n_f)),
        dma((n_f,)), dma((n_f,)),
        dma((n_c // n_t, n_t)), dma((n_c // n_t, n_t)),
        dma((n_c, PIECES)), dma((n_c, PIECES)), dma((n_c, PIECES)), dma((n_c, PIECES)), dma((n_c, PIECES)),
        dma((n_ft,)), dma((n_ft,)),
        dma((8,)), dma((n_c,)), dma((n_c // n_t,)),
    ]
    held = pl.pallas_call(
        functools.partial(kernel, n_g, n_f, n_t, n_c),
        out_shape=(
            pltpu.VMEM(weight.shape, bf16),
            pltpu.VMEM(weight.shape, f32),
            pltpu.VMEM(weight.shape, f32),
            pltpu.VMEM((ATT_PARTS, n_q, HEAD_DIM), f32),
            pltpu.VMEM((ATT_PARTS, n_q, STEPS * row_dev), bf16),
            pltpu.VMEM((STEPS * row_dev, n_t * width), bf16),
        ),
        in_specs=[pl.BlockSpec(memory_space=pltpu.SMEM)] + [anywhere] * 10,
        out_specs=(pl.BlockSpec(memory_space=pltpu.VMEM),) * 6,
        scratch_shapes=scratch,
        compiler_params=pltpu.CompilerParams(
            collective_id=0, has_side_effects=True, vmem_limit_bytes=48 * 1024 * 1024
        ),
        name="step",
    )(
        lengths, tokens, cotangent, weight, moment_one, moment_two, hidden, queries, new_keys,
        key_cache, value_cache,
    )
    return finish(queries.shape, *held)


def solution(mesh):
    in_specs = (
        P(("group", "fsdp"), None),
        P(("group", "fsdp"), "tensor"),
        P("fsdp", "tensor"),
        P("fsdp", "tensor"),
        P("fsdp", "tensor"),
        P(None, "group", ("fsdp", "tensor")),
        P(None, ("group", "fsdp", "tensor"), None),
        P(None, ("group", "fsdp", "tensor"), None),
        P(("group", "fsdp", "tensor"), None, None),
        P(("group", "fsdp", "tensor"), None, None),
        P(("group", "fsdp", "tensor")),
    )
    out_specs = (
        P("fsdp", "tensor"),
        P("fsdp", "tensor"),
        P("fsdp", "tensor"),
        P(None, ("group", "fsdp", "tensor"), None),
    )
    sizes = (mesh.shape["group"], mesh.shape["fsdp"], mesh.shape["tensor"])
    return jax.shard_map(
        functools.partial(per_device, *sizes),
        mesh=mesh, in_specs=in_specs, out_specs=out_specs, check_vma=False,
    )
```

```python
import functools

import jax
import jax.numpy as jnp
from jax import lax
from jax.experimental import pallas as pl
from jax.experimental.pallas import tpu as pltpu
from jax.sharding import PartitionSpec as P

HEAD_DIM = 128
GROUP_HEADS = 8
KV_HEADS = 4
STEPS = 4
ADAM_STEP = 10

CHUNKS = 16
PIECES = 2
IN_LAG = 1
MID_LAG = 3
OUT_LAG = 4
ATT_PARTS = 8
ATT_FIRST = 4
AHEAD = 3

learn_rate = 0.001
beta_one = 0.9
beta_two = 0.95
epsilon = 1e-08
decay_rate = 0.1
masked_score = -1e30

MESH = pl.DeviceIdType.MESH


def adamw(gradient, weight, moment_one, moment_two):
    first_new = beta_one * moment_one + (1.0 - beta_one) * gradient
    second_new = beta_two * moment_two + (1.0 - beta_two) * gradient * gradient
    first_hat = first_new * (1.0 / (1.0 - beta_one**ADAM_STEP))
    second_hat = second_new * (1.0 / (1.0 - beta_two**ADAM_STEP))
    stepped = weight.astype(jnp.float32) * (
        1.0 - learn_rate * decay_rate
    ) - learn_rate * first_hat / (jnp.sqrt(second_hat) + epsilon)
    return stepped.astype(jnp.bfloat16), first_new, second_new


def kernel(
    n_g, n_f, n_t, n_c,
    lens, tokens, cot, weight, mom1, mom2, hidden, queries, new_keys, kcache, vcache,
    w_v, m1_v, m2_v, oc, pf, fresh,
    tok, cots, hid, own, sb, r1, r2, gt, q_v, nk_v, kc_v, vc_v,
    acc, ps, pr,
    tok_s, tok_r, cot_s, cot_r, hid_s, hid_r, in_s, out_s, r1_r, back_r,
    pr_s, pr_r, loc,
):
    g = lax.axis_index("group")
    f = lax.axis_index("fsdp")
    t = lax.axis_index("tensor")
    n_ft = n_f * n_t
    me = f * n_t + t
    rows_c = tok.shape[3]
    rows = n_c * rows_c
    per_t = n_c // n_t
    row_dev = kc_v.shape[0]
    cache = kc_v.shape[1]
    width = cot.shape[1]

    mid_l, mid_r = n_g // 2 - 1, n_g // 2
    on_left = g <= mid_l
    toward = jnp.where(on_left, 1, -1)
    depth = jnp.where(on_left, g, n_g - 1 - g)
    mid_depth = jnp.where(on_left, mid_l, n_g - 1 - mid_r)
    is_mid = depth == mid_depth
    max_depth = max(mid_l, n_g - 1 - mid_r)

    barrier = pltpu.get_barrier_semaphore()
    for k in range(1, n_ft):
        peer = lax.rem(me + k, n_ft)
        pl.semaphore_signal(
            barrier, inc=1, device_id={"fsdp": peer // n_t, "tensor": peer % n_t}, device_id_type=MESH
        )

    def tell(to):
        pl.semaphore_signal(
            barrier, inc=1, device_id={"group": lax.rem(g + to + n_g, n_g)}, device_id_type=MESH
        )

    @pl.when(is_mid)
    def _():
        tell(toward)

    def local(src, dst, sem):
        copy = pltpu.make_async_copy(src, dst, sem)
        copy.start()
        return copy

    def row_block(c):
        return lax.rem(c + t * per_t, n_c)

    def tok_local(c):
        col = pl.multiple_of(f * rows + row_block(c) * rows_c, rows_c)
        return pltpu.make_async_copy(tokens.at[:, pl.ds(col, rows_c)], tok.at[c, 0], tok_r.at[c])

    def hid_local(j):
        return pltpu.make_async_copy(
            hidden.at[:, :, pl.ds(j * rows_c, rows_c)], hid.at[t * per_t + j], hid_r.at[t * per_t + j]
        )

    cot_l = local(cot, cots.at[0], loc.at[0])
    loads_att = [
        local(queries, q_v, loc.at[1]),
        local(new_keys, nk_v, loc.at[2]),
        local(kcache, kc_v, loc.at[3]),
        local(vcache, vc_v, loc.at[4]),
    ]
    for c in range(AHEAD):
        tok_local(c).start()

    @pl.when((depth == 0) & jnp.logical_not(is_mid))
    def _():
        pl.semaphore_wait(barrier, n_ft - 1)

    @pl.when((depth == 0) & is_mid)
    def _():
        pl.semaphore_wait(barrier, n_ft)

    @pl.when((depth > 0) & jnp.logical_not(is_mid))
    def _():
        pl.semaphore_wait(barrier, n_ft)
        tell(-toward)

    @pl.when((depth > 0) & is_mid)
    def _():
        pl.semaphore_wait(barrier, n_ft + 1)
        tell(-toward)

    @pl.when(jnp.logical_not(is_mid))
    def _():
        tell(toward)

    def fsdp_peer(k):
        return (f // 2 * 2 + k // 2 * 2) % n_f + (f % 2 + k % 2) % 2

    def cot_copy(k):
        return pltpu.make_async_remote_copy(
            src_ref=cots.at[k - 1] if k % 2 else cot, dst_ref=cots.at[k],
            send_sem=cot_s.at[k], recv_sem=cot_r.at[k],
            device_id={"fsdp": fsdp_peer(1 if k % 2 else k)}, device_id_type=MESH,
        )

    def tok_copy(c, k):
        peer = fsdp_peer(k)
        col = pl.multiple_of(peer * rows + row_block(c) * rows_c, rows_c)
        return pltpu.make_async_remote_copy(
            src_ref=tokens.at[:, pl.ds(col, rows_c)], dst_ref=tok.at[c, k],
            send_sem=tok_s.at[0], recv_sem=tok_r.at[c],
            device_id={"fsdp": peer}, device_id_type=MESH,
        )

    def hid_copy(j, k):
        return pltpu.make_async_remote_copy(
            src_ref=hidden.at[:, :, pl.ds(j * rows_c, rows_c)], dst_ref=hid.at[t * per_t + j],
            send_sem=hid_s.at[0], recv_sem=hid_r.at[t * per_t + j],
            device_id={"tensor": lax.rem(t + k, n_t)}, device_id_type=MESH,
        )

    def arrived(ref, sem):
        pltpu.make_async_copy(ref, ref, sem).wait()

    def send_tokens(c):
        for k in range(n_f - 1, 0, -1):
            tok_copy(c, k).start()

    for k in range(2, n_f, 2):
        cot_copy(k).start()
    cot_l.wait()
    cot_copy(1).start()
    for c in range(AHEAD):
        send_tokens(c)

    loads_adam = [
        local(weight, w_v, loc.at[5]),
        local(mom1, m1_v, loc.at[6]),
        local(mom2, m2_v, loc.at[7]),
    ]
    for copy in loads_att:
        copy.wait()

    heads_part = KV_HEADS * GROUP_HEADS // ATT_PARTS

    def attend(part):
        h = part * heads_part // GROUP_HEADS
        qs = [
            q_v[:, :, pl.ds(pl.multiple_of((part * heads_part + j) * HEAD_DIM, HEAD_DIM), HEAD_DIM)]
            .reshape(STEPS * row_dev, HEAD_DIM)
            for j in range(heads_part)
        ]
        q = jnp.concatenate(qs, axis=0)
        cols = pl.ds(pl.multiple_of(h * HEAD_DIM, HEAD_DIM), HEAD_DIM)
        kk = kc_v[:, :, cols].reshape(row_dev * cache, HEAD_DIM)
        fk = nk_v[:, :, cols].reshape(STEPS * row_dev, HEAD_DIM)
        vv = vc_v[:, :, cols].reshape(row_dev * cache, HEAD_DIM)
        contract = (((1,), (1,)), ((), ()))
        scale = HEAD_DIM ** (-0.5)
        s_c = lax.dot_general(q, kk, contract, preferred_element_type=jnp.float32) * scale
        s_f = lax.dot_general(q, fk, contract, preferred_element_type=jnp.float32) * scale
        n_q = q.shape[0]
        col_c = lax.broadcasted_iota(jnp.int32, (1, row_dev * cache), 1)
        col_row = col_c // cache
        limit = jnp.zeros_like(col_c)
        for r in range(row_dev):
            limit = jnp.where(col_row == r, lens[r], limit)
        col_row = jnp.where(col_c % cache < limit, col_row, -1)
        q_id = lax.broadcasted_iota(jnp.int32, (n_q, 1), 0)
        q_row = q_id % row_dev
        q_step = (q_id // row_dev) % STEPS
        col_f = lax.broadcasted_iota(jnp.int32, (1, STEPS * row_dev), 1)
        ok_c = q_row == col_row
        ok_f = (q_row == col_f % row_dev) & (col_f // row_dev <= q_step)
        s_c = jnp.where(ok_c, s_c, masked_score)
        s_f = jnp.where(ok_f, s_f, masked_score)
        highest = jnp.maximum(
            jnp.max(s_c, axis=-1, keepdims=True), jnp.max(s_f, axis=-1, keepdims=True)
        )
        e_c = jnp.exp(s_c - highest)
        e_f = jnp.exp(s_f - highest)
        den = jnp.sum(e_c, axis=-1, keepdims=True) + jnp.sum(e_f, axis=-1, keepdims=True)
        p_c = (e_c / den).astype(jnp.bfloat16)
        pf[part] = (e_f / den).astype(jnp.bfloat16)
        oc[part] = jnp.dot(p_c, vv, preferred_element_type=jnp.float32)

    for part in range(ATT_FIRST // 2):
        attend(part)
    for k in range(2, n_f, 2):
        cot_copy(k).wait_recv()
        cot_copy(k + 1).start()
    for part in range(ATT_FIRST // 2, ATT_FIRST):
        attend(part)
    acc[...] = jnp.zeros_like(acc)
    for k in range(1, n_f, 2):
        cot_copy(k).wait_recv()

    @pl.when(jnp.logical_not(is_mid))
    def _():
        pl.semaphore_wait(barrier, 1)

    def inward(c, p, dst, recv):
        return pltpu.make_async_remote_copy(
            src_ref=sb.at[c, p], dst_ref=dst.at[c, p], send_sem=in_s.at[0], recv_sem=recv.at[c, p],
            device_id={"group": lax.rem(g + toward + n_g, n_g)}, device_id_type=MESH,
        )

    def outward(c, p):
        return pltpu.make_async_remote_copy(
            src_ref=gt.at[c, p], dst_ref=gt.at[c, p], send_sem=out_s.at[0], recv_sem=back_r.at[c, p],
            device_id={"group": lax.rem(g - toward + n_g, n_g)}, device_id_type=MESH,
        )

    def send_inward(c, p, part):
        sb[c, p] = part.astype(jnp.bfloat16)

        @pl.when(is_mid)
        def _():
            inward(c, p, r2, back_r).start()

        @pl.when(jnp.logical_not(is_mid))
        def _():
            inward(c, p, r1, r1_r).start()

    def active(c):
        return (c >= 0) & (c < n_c)

    pieces, piece = sb.shape[1:3]
    first_total = IN_LAG * max_depth + MID_LAG

    def slot(s, carry):
        @pl.when(s < n_c - AHEAD)
        def _():
            tok_local(s + AHEAD).start()
            send_tokens(s + AHEAD)

        @pl.when(s < per_t)
        def _():
            for k in range(1, n_t):
                hid_copy(s, k).start()
            hid_local(s).start()

        @pl.when(s < n_c)
        def _():
            arrived(tok.at[s], tok_r.at[s])
            grad = lax.dot_general(
                tok[s].reshape(n_f * tok.shape[2], rows_c),
                cots[...].reshape(n_f * tok.shape[2], width), (((0,), (0,)), ((), ())),
                preferred_element_type=jnp.float32,
            )

            @pl.when(depth == 0)
            def _():
                for p in range(pieces):
                    send_inward(s, p, grad[p * piece : (p + 1) * piece])

            @pl.when(depth > 0)
            def _():
                for p in range(pieces):
                    own[s, p] = grad[p * piece : (p + 1) * piece]

        c1 = s - IN_LAG * depth

        @pl.when((depth > 0) & active(c1))
        def _():
            for p in range(pieces):
                inward(c1, p, r1, r1_r).wait_recv()
                send_inward(c1, p, own[c1, p] + r1[c1, p].astype(jnp.float32))

        @pl.when(s == first_total)
        def _():
            for copy in loads_adam:
                copy.wait()

        c2 = s - first_total - OUT_LAG * (mid_depth - depth)

        @pl.when(active(c2))
        def _():
            @pl.when(is_mid)
            def _():
                for p in range(pieces):
                    inward(c2, p, r2, back_r).wait_recv()
                    total = sb[c2, p].astype(jnp.float32) + r2[c2, p].astype(jnp.float32)
                    gt[c2, p] = total.astype(jnp.bfloat16)

                    @pl.when(depth > 0)
                    def _():
                        outward(c2, p).start()

            @pl.when(jnp.logical_not(is_mid))
            def _():
                for p in range(pieces):
                    outward(c2, p).wait_recv()

                    @pl.when(depth > 0)
                    def _():
                        outward(c2, p).start()

            b = row_block(c2)

            arrived(hid.at[b], hid_r.at[b])
            span = pl.ds(pl.multiple_of(b * rows_c, rows_c), rows_c)
            w_new, m1_new, m2_new = adamw(
                gt[c2].reshape(rows_c, width).astype(jnp.float32), w_v[span], m1_v[span], m2_v[span]
            )
            w_v[span] = w_new
            m1_v[span] = m1_new
            m2_v[span] = m2_new
            lhs = hid[b].reshape(acc.shape[0], rows_c)
            acc[...] += jnp.dot(lhs, w_new, preferred_element_type=jnp.float32)

        @pl.when(s < ATT_PARTS - ATT_FIRST)
        def _():
            attend(s + ATT_FIRST)

        return carry

    slots = n_c + first_total + OUT_LAG * max_depth
    lax.fori_loop(0, max(slots, ATT_PARTS - ATT_FIRST), slot, 0)

    def out_copy(k):
        peer = lax.rem(me + k, n_ft)
        return pltpu.make_async_remote_copy(
            src_ref=ps.at[k], dst_ref=pr.at[t * n_f + f], send_sem=pr_s.at[0], recv_sem=pr_r.at[0],
            device_id={"fsdp": peer // n_t, "tensor": peer % n_t}, device_id_type=MESH,
        )

    ps_all = acc.reshape(STEPS, acc.shape[0] // STEPS, width)
    for k in range(1, n_ft):
        peer = lax.rem(me + k, n_ft)
        take = pl.ds(pl.multiple_of(peer * row_dev, row_dev), row_dev)
        ps[k] = ps_all[:, take, :].reshape(STEPS * row_dev, width).astype(jnp.bfloat16)
        out_copy(k).start()
    take = pl.ds(pl.multiple_of(me * row_dev, row_dev), row_dev)
    pr[t * n_f + f] = ps_all[:, take, :].reshape(STEPS * row_dev, width).astype(jnp.bfloat16)
    for k in range(1, n_f):
        cot_copy(k).wait_send()
    arrived(tok.at[:, pl.ds(1, n_f - 1)], tok_s.at[0])
    arrived(hid.at[pl.ds(0, per_t * (n_t - 1))], hid_s.at[0])
    arrived(sb, in_s.at[0])

    @pl.when(depth > 0)
    def _():
        arrived(gt, out_s.at[0])

    arrived(pr.at[pl.ds(0, n_ft - 1)], pr_r.at[0])
    fresh_parts = []
    for tt in range(n_t):
        total = pr[tt * n_f].astype(jnp.float32)
        for ff in range(1, n_f):
            total = total + pr[tt * n_f + ff].astype(jnp.float32)
        fresh_parts.append(total.astype(jnp.bfloat16))
    fresh[...] = jnp.concatenate(fresh_parts, axis=1)

    arrived(ps.at[pl.ds(0, n_ft - 1)], pr_s.at[0])


def finish_kernel(w_v, m1_v, m2_v, oc, pf, fresh, w_o, m1_o, m2_o, att_o, att_v, sems):
    copies = []
    for a, o, cuts in ((m1_v, m1_o, 4), (m2_v, m2_o, 4), (w_v, w_o, 2)):
        rows = a.shape[0] // cuts
        for j in range(cuts):
            span = pl.ds(j * rows, rows)
            copies.append(pltpu.make_async_copy(a.at[span], o.at[span], sems.at[len(copies)]))
            copies[-1].start()
    heads_part = KV_HEADS * GROUP_HEADS // ATT_PARTS
    steps, row_dev = att_v.shape[:2]
    block = steps * row_dev
    for part in range(ATT_PARTS):
        h = part * heads_part // GROUP_HEADS
        res = oc[part] + jnp.dot(
            pf[part], fresh[:, h * HEAD_DIM : (h + 1) * HEAD_DIM], preferred_element_type=jnp.float32
        )
        for j in range(heads_part):
            at = (part * heads_part + j) * HEAD_DIM
            att_v[:, :, at : at + HEAD_DIM] = (
                res[j * block : (j + 1) * block].reshape(steps, row_dev, HEAD_DIM).astype(jnp.bfloat16)
            )
        cols = pl.ds(part * heads_part * HEAD_DIM, heads_part * HEAD_DIM)
        copies.append(
            pltpu.make_async_copy(att_v.at[:, :, cols], att_o.at[:, :, cols], sems.at[len(copies)])
        )
        copies[-1].start()
    for copy in copies:
        copy.wait()


def finish(att_shape, w, m1, m2, *rest):
    spec = pl.BlockSpec(memory_space=pl.ANY)
    outs = [jax.ShapeDtypeStruct(a.shape, a.dtype) for a in (w, m1, m2)]
    outs.append(jax.ShapeDtypeStruct(att_shape, jnp.bfloat16))
    held = [pltpu.with_memory_space_constraint(a, pltpu.VMEM) for a in (w, m1, m2) + rest]
    return pl.pallas_call(
        finish_kernel,
        out_shape=tuple(outs),
        in_specs=[pl.BlockSpec(memory_space=pltpu.VMEM)] * len(held),
        out_specs=(spec,) * 4,
        scratch_shapes=[pltpu.VMEM(att_shape, jnp.bfloat16), pltpu.SemaphoreType.DMA((10 + ATT_PARTS,))],
        compiler_params=pltpu.CompilerParams(vmem_limit_bytes=16 * 1024 * 1024),
        name="finish",
    )(*held)


def per_device(
    n_g, n_f, n_t,
    tokens, cotangent, weight, moment_one, moment_two, hidden, queries, new_keys,
    key_cache, value_cache, lengths,
):
    n_ft = n_f * n_t
    rows, width = weight.shape
    n_c = max(CHUNKS, n_t)
    rows_c = rows // n_c
    row_dev, cache, kvw = key_cache.shape
    tok_rows = tokens.shape[0]
    piece_shape = (n_c, PIECES, rows_c // PIECES, width)
    acc_rows = hidden.shape[0] * hidden.shape[1]
    n_q = KV_HEADS * GROUP_HEADS // ATT_PARTS * STEPS * row_dev
    bf16, f32 = jnp.bfloat16, jnp.float32
    dma = pltpu.SemaphoreType.DMA
    anywhere = pl.BlockSpec(memory_space=pl.ANY)
    scratch = [
        pltpu.VMEM((n_c, n_f, tok_rows, rows_c), bf16),
        pltpu.VMEM((n_f, tok_rows, width), bf16),
        pltpu.VMEM((n_c,) + hidden.shape[:2] + (rows_c,), bf16),
        pltpu.VMEM(piece_shape, f32),
        pltpu.VMEM(piece_shape, bf16),
        pltpu.VMEM(piece_shape, bf16),
        pltpu.VMEM(piece_shape, bf16),
        pltpu.VMEM(piece_shape, bf16),
        pltpu.VMEM(queries.shape, bf16),
        pltpu.VMEM(new_keys.shape, bf16),
        pltpu.VMEM(key_cache.shape, bf16),
        pltpu.VMEM(value_cache.shape, bf16),
        pltpu.VMEM((acc_rows, width), f32),
        pltpu.VMEM((n_ft, STEPS * row_dev, width), bf16),
        pltpu.VMEM((n_ft, STEPS * row_dev, width), bf16),
        dma((1,)), dma((n_c,)),
        dma((n_f,)), dma((n_f,)),
        dma((1,)), dma((n_c,)),
        dma((1,)), dma((1,)), dma((n_c, PIECES)), dma((n_c, PIECES)),
        dma((1,)), dma((1,)), dma((8,)),
    ]
    held = pl.pallas_call(
        functools.partial(kernel, n_g, n_f, n_t, n_c),
        out_shape=(
            pltpu.VMEM(weight.shape, bf16),
            pltpu.VMEM(weight.shape, f32),
            pltpu.VMEM(weight.shape, f32),
            pltpu.VMEM((ATT_PARTS, n_q, HEAD_DIM), f32),
            pltpu.VMEM((ATT_PARTS, n_q, STEPS * row_dev), bf16),
            pltpu.VMEM((STEPS * row_dev, n_t * width), bf16),
        ),
        in_specs=[pl.BlockSpec(memory_space=pltpu.SMEM)] + [anywhere] * 10,
        out_specs=(pl.BlockSpec(memory_space=pltpu.VMEM),) * 6,
        scratch_shapes=scratch,
        compiler_params=pltpu.CompilerParams(
            collective_id=0, has_side_effects=True, vmem_limit_bytes=48 * 1024 * 1024
        ),
        name="step",
    )(
        lengths, tokens, cotangent, weight, moment_one, moment_two, hidden, queries, new_keys,
        key_cache, value_cache,
    )
    return finish(queries.shape, *held)


def solution(mesh):
    in_specs = (
        P(("group", "fsdp"), None),
        P(("group", "fsdp"), "tensor"),
        P("fsdp", "tensor"),
        P("fsdp", "tensor"),
        P("fsdp", "tensor"),
        P(None, "group", ("fsdp", "tensor")),
        P(None, ("group", "fsdp", "tensor"), None),
        P(None, ("group", "fsdp", "tensor"), None),
        P(("group", "fsdp", "tensor"), None, None),
        P(("group", "fsdp", "tensor"), None, None),
        P(("group", "fsdp", "tensor")),
    )
    out_specs = (
        P("fsdp", "tensor"),
        P("fsdp", "tensor"),
        P("fsdp", "tensor"),
        P(None, ("group", "fsdp", "tensor"), None),
    )
    sizes = (mesh.shape["group"], mesh.shape["fsdp"], mesh.shape["tensor"])
    return jax.shard_map(
        functools.partial(per_device, *sizes),
        mesh=mesh, in_specs=in_specs, out_specs=out_specs, check_vma=False,
    )
```

```python
import functools

import jax
import jax.numpy as jnp
from jax import lax
from jax.experimental import pallas as pl
from jax.experimental.pallas import tpu as pltpu
from jax.sharding import PartitionSpec as P

HEAD_DIM = 128
GROUP_HEADS = 8
KV_HEADS = 4
STEPS = 4
ADAM_STEP = 10

CHUNKS = 16
PIECES = 2
IN_LAG = 1
MID_LAG = 3
OUT_LAG = 4
ATT_PARTS = 8
MID_ATT_SLOTS = (0, 0, 0, 0, 10, 11, 12, 13)
END_ATT_SLOTS = (1, 1, 3, 4, 5, 12, 13, 14)
AHEAD = 4
EARLY_WAIT = 4

learn_rate = 0.001
beta_one = 0.9
beta_two = 0.95
epsilon = 1e-08
decay_rate = 0.1
masked_score = -1e30

MESH = pl.DeviceIdType.MESH


def adamw(gradient, weight, moment_one, moment_two):
    first_new = beta_one * moment_one + (1.0 - beta_one) * gradient
    second_new = beta_two * moment_two + (1.0 - beta_two) * gradient * gradient
    first_hat = first_new * (1.0 / (1.0 - beta_one**ADAM_STEP))
    second_hat = second_new * (1.0 / (1.0 - beta_two**ADAM_STEP))
    stepped = weight.astype(jnp.float32) * (
        1.0 - learn_rate * decay_rate
    ) - learn_rate * first_hat / (jnp.sqrt(second_hat) + epsilon)
    return stepped.astype(jnp.bfloat16), first_new, second_new


def kernel(
    n_g, n_f, n_t, n_c, early,
    lens, tokens, cot, weight, mom1, mom2, hidden, queries, new_keys, kcache, vcache,
    w_v, m1_v, m2_v, oc, pf, fresh,
    tok, cots, hid, own, sb, r1, r2, gt, other, q_v, nk_v, kc_v, vc_v,
    acc, ps, pr,
    tok_s, tok_r, cot_s, cot_r, hid_s, hid_r, in_s, out_s, r1_r, back_r, other_s, other_r,
    pr_s, pr_r, loc,
):
    g = lax.axis_index("group")
    f = lax.axis_index("fsdp")
    t = lax.axis_index("tensor")
    n_ft = n_f * n_t
    me = f * n_t + t
    rows_c = tok.shape[3]
    rows = n_c * rows_c
    per_t = n_c // n_t
    n_z = n_c + early
    row_dev = kc_v.shape[0]
    cache = kc_v.shape[1]
    width = cot.shape[1]

    mid_l, mid_r = n_g // 2 - 1, n_g // 2
    on_left = g <= mid_l
    toward = jnp.where(on_left, 1, -1)
    depth = jnp.where(on_left, g, n_g - 1 - g)
    mid_depth = jnp.where(on_left, mid_l, n_g - 1 - mid_r)
    is_mid = depth == mid_depth
    max_depth = max(mid_l, n_g - 1 - mid_r)

    barrier = pltpu.get_barrier_semaphore()
    for k in range(1, n_ft):
        peer = lax.rem(me + k, n_ft)
        pl.semaphore_signal(
            barrier, inc=1, device_id={"fsdp": peer // n_t, "tensor": peer % n_t}, device_id_type=MESH
        )

    def tell(to):
        pl.semaphore_signal(
            barrier, inc=1, device_id={"group": lax.rem(g + to + n_g, n_g)}, device_id_type=MESH
        )

    @pl.when(is_mid)
    def _():
        tell(toward)

    def local(src, dst, sem):
        copy = pltpu.make_async_copy(src, dst, sem)
        copy.start()
        return copy

    def row_block(c):
        return lax.rem(jnp.maximum(c - early, 0) + t * per_t, n_c)

    def across(i):
        return (i // 2 * 2 + 2) % n_f + i % 2

    def tok_column(c, to):
        owner = jnp.where(c == 1, across(to), to) if early else to
        return pl.multiple_of(owner * rows + row_block(c) * rows_c, rows_c)

    def tok_local(c):
        return pltpu.make_async_copy(
            tokens.at[:, pl.ds(tok_column(c, f), rows_c)], tok.at[c, 0], tok_r.at[c]
        )

    def hid_local(j):
        return pltpu.make_async_copy(
            hidden.at[:, :, pl.ds(j * rows_c, rows_c)], hid.at[t * per_t + j], hid_r.at[t * per_t + j]
        )

    cot_l = local(cot, cots.at[0], loc.at[0])
    loads_att = [
        local(queries, q_v, loc.at[1]),
        local(new_keys, nk_v, loc.at[2]),
        local(kcache, kc_v, loc.at[3]),
        local(vcache, vc_v, loc.at[4]),
    ]
    for c in range(AHEAD):
        tok_local(c).start()

    @pl.when((depth == 0) & jnp.logical_not(is_mid))
    def _():
        pl.semaphore_wait(barrier, n_ft - 1)

    @pl.when((depth == 0) & is_mid)
    def _():
        pl.semaphore_wait(barrier, n_ft)

    @pl.when((depth > 0) & jnp.logical_not(is_mid))
    def _():
        pl.semaphore_wait(barrier, n_ft)
        tell(-toward)

    @pl.when((depth > 0) & is_mid)
    def _():
        pl.semaphore_wait(barrier, n_ft + 1)
        tell(-toward)

    @pl.when(jnp.logical_not(is_mid))
    def _():
        tell(toward)

    def fsdp_peer(k):
        return (f // 2 * 2 + k // 2 * 2) % n_f + (f % 2 + k % 2) % 2

    def cot_copy(k):
        return pltpu.make_async_remote_copy(
            src_ref=cots.at[k - 1] if k % 2 and k > 1 else cot, dst_ref=cots.at[k],
            send_sem=cot_s.at[k], recv_sem=cot_r.at[k],
            device_id={"fsdp": fsdp_peer(1 if k % 2 else k)}, device_id_type=MESH,
        )

    def tok_copy(c, k):
        peer = fsdp_peer(k)
        return pltpu.make_async_remote_copy(
            src_ref=tokens.at[:, pl.ds(tok_column(c, peer), rows_c)], dst_ref=tok.at[c, k],
            send_sem=tok_s.at[min(k, 2) - 1], recv_sem=tok_r.at[c],
            device_id={"fsdp": peer}, device_id_type=MESH,
        )

    def hid_copy(j, k):
        return pltpu.make_async_remote_copy(
            src_ref=hidden.at[:, :, pl.ds(j * rows_c, rows_c)], dst_ref=hid.at[t * per_t + j],
            send_sem=hid_s.at[0], recv_sem=hid_r.at[t * per_t + j],
            device_id={"tensor": lax.rem(t + k, n_t)}, device_id_type=MESH,
        )

    def arrived(ref, sem):
        pltpu.make_async_copy(ref, ref, sem).wait()

    def send_tokens(c):
        @pl.when((early == 0) | (c >= 2))
        def _():
            for k in range(n_f - 1, 1, -1):
                tok_copy(c, k).start()

        tok_copy(c, 1).start()

    for k in range(2, n_f, 2):
        cot_copy(k).start()
    cot_copy(1).start()
    for c in range(AHEAD):
        send_tokens(c)

    loads_adam = [
        local(weight, w_v, loc.at[5]),
        local(mom1, m1_v, loc.at[6]),
        local(mom2, m2_v, loc.at[7]),
    ]
    for copy in loads_att:
        copy.wait()

    heads_part = KV_HEADS * GROUP_HEADS // ATT_PARTS

    def attend(part):
        h = part * heads_part // GROUP_HEADS
        qs = [
            q_v[:, :, pl.ds(pl.multiple_of((part * heads_part + j) * HEAD_DIM, HEAD_DIM), HEAD_DIM)]
            .reshape(STEPS * row_dev, HEAD_DIM)
            for j in range(heads_part)
        ]
        q = jnp.concatenate(qs, axis=0)
        cols = pl.ds(pl.multiple_of(h * HEAD_DIM, HEAD_DIM), HEAD_DIM)
        kk = kc_v[:, :, cols].reshape(row_dev * cache, HEAD_DIM)
        fk = nk_v[:, :, cols].reshape(STEPS * row_dev, HEAD_DIM)
        vv = vc_v[:, :, cols].reshape(row_dev * cache, HEAD_DIM)
        contract = (((1,), (1,)), ((), ()))
        scale = HEAD_DIM ** (-0.5)
        s_c = lax.dot_general(q, kk, contract, preferred_element_type=jnp.float32) * scale
        s_f = lax.dot_general(q, fk, contract, preferred_element_type=jnp.float32) * scale
        n_q = q.shape[0]
        col_c = lax.broadcasted_iota(jnp.int32, (1, row_dev * cache), 1)
        col_row = col_c // cache
        limit = jnp.zeros_like(col_c)
        for r in range(row_dev):
            limit = jnp.where(col_row == r, lens[r], limit)
        col_row = jnp.where(col_c % cache < limit, col_row, -1)
        q_id = lax.broadcasted_iota(jnp.int32, (n_q, 1), 0)
        q_row = q_id % row_dev
        q_step = (q_id // row_dev) % STEPS
        col_f = lax.broadcasted_iota(jnp.int32, (1, STEPS * row_dev), 1)
        ok_c = q_row == col_row
        ok_f = (q_row == col_f % row_dev) & (col_f // row_dev <= q_step)
        s_c = jnp.where(ok_c, s_c, masked_score)
        s_f = jnp.where(ok_f, s_f, masked_score)
        highest = jnp.maximum(
            jnp.max(s_c, axis=-1, keepdims=True), jnp.max(s_f, axis=-1, keepdims=True)
        )
        e_c = jnp.exp(s_c - highest)
        e_f = jnp.exp(s_f - highest)
        den = jnp.sum(e_c, axis=-1, keepdims=True) + jnp.sum(e_f, axis=-1, keepdims=True)
        p_c = (e_c / den).astype(jnp.bfloat16)
        pf[part] = (e_f / den).astype(jnp.bfloat16)
        oc[part] = jnp.dot(p_c, vv, preferred_element_type=jnp.float32)

    acc[...] = jnp.zeros_like(acc)
    cot_l.wait()
    cot_copy(1).wait_recv()

    def cot_rest():
        for k in range(2, n_f, 2):
            cot_copy(k).wait_recv()
            cot_copy(k + 1).start()

    def cot_ready():
        for k in range(3, n_f, 2):
            cot_copy(k).wait_recv()

    if not early:
        cot_rest()
        cot_ready()

    @pl.when(jnp.logical_not(is_mid))
    def _():
        pl.semaphore_wait(barrier, 1)

    def parts_done(s):
        mid = sum((s >= at).astype(jnp.int32) for at in MID_ATT_SLOTS)
        end = sum((s >= at).astype(jnp.int32) for at in END_ATT_SLOTS)
        return jnp.where(is_mid, mid, end)

    def inward(c, p, dst, recv):
        return pltpu.make_async_remote_copy(
            src_ref=sb.at[c, p], dst_ref=dst.at[c, p], send_sem=in_s.at[0], recv_sem=recv.at[c, p],
            device_id={"group": lax.rem(g + toward + n_g, n_g)}, device_id_type=MESH,
        )

    def outward(c, p):
        return pltpu.make_async_remote_copy(
            src_ref=gt.at[c, p], dst_ref=gt.at[c, p], send_sem=out_s.at[0], recv_sem=back_r.at[c, p],
            device_id={"group": lax.rem(g - toward + n_g, n_g)}, device_id_type=MESH,
        )

    def send_inward(c, p, part):
        sb[c, p] = part.astype(jnp.bfloat16)

        @pl.when(is_mid)
        def _():
            inward(c, p, r2, back_r).start()

        @pl.when(jnp.logical_not(is_mid))
        def _():
            inward(c, p, r1, r1_r).start()

    def active(c):
        return (c >= 0) & (c < n_z)

    def to_other():
        return pltpu.make_async_remote_copy(
            src_ref=gt.at[1], dst_ref=other, send_sem=other_s.at[0], recv_sem=other_r.at[0],
            device_id={"fsdp": fsdp_peer(2)}, device_id_type=MESH,
        )

    pieces, piece = sb.shape[1:3]
    first_total = IN_LAG * max_depth + MID_LAG

    def gradient(block, cot_block):
        k = block.shape[0] * block.shape[1]
        return lax.dot_general(
            block.reshape(k, rows_c), cot_block.reshape(k, width), (((0,), (0,)), ((), ())),
            preferred_element_type=jnp.float32,
        )

    def place(s, grad):
        @pl.when(depth == 0)
        def _():
            for p in range(pieces):
                send_inward(s, p, grad[p * piece : (p + 1) * piece])

        @pl.when(depth > 0)
        def _():
            for p in range(pieces):
                own[s, p] = grad[p * piece : (p + 1) * piece]

    def update(b, grad):
        arrived(hid.at[b], hid_r.at[b])
        span = pl.ds(pl.multiple_of(b * rows_c, rows_c), rows_c)
        w_new, m1_new, m2_new = adamw(
            grad.reshape(rows_c, width), w_v[span], m1_v[span], m2_v[span]
        )
        w_v[span] = w_new
        m1_v[span] = m1_new
        m2_v[span] = m2_new
        lhs = hid[b].reshape(acc.shape[0], rows_c)
        acc[...] += jnp.dot(lhs, w_new, preferred_element_type=jnp.float32)

    last_total = first_total + OUT_LAG * max_depth
    to_other_at = max(n_z - 1, last_total + 1)
    early_at = to_other_at + EARLY_WAIT

    def slot(s, carry):
        @pl.when(s < n_z - AHEAD)
        def _():
            tok_local(s + AHEAD).start()
            send_tokens(s + AHEAD)

        @pl.when(s < per_t)
        def _():
            for k in range(1, n_t):
                hid_copy(s, k).start()
            hid_local(s).start()

        if early:

            @pl.when(s < 2)
            def _():
                arrived(tok.at[s, pl.ds(0, 2)], tok_r.at[s])
                place(s, gradient(tok[s, 0:2], cots[0:2]))

            @pl.when(s == 2)
            def _():
                cot_ready()

        @pl.when((s >= 2 * early) & (s < n_z))
        def _():
            arrived(tok.at[s], tok_r.at[s])
            place(s, gradient(tok[s], cots[...]))

        c1 = s - IN_LAG * depth

        @pl.when((depth > 0) & active(c1))
        def _():
            for p in range(pieces):
                inward(c1, p, r1, r1_r).wait_recv()
                send_inward(c1, p, own[c1, p] + r1[c1, p].astype(jnp.float32))

        @pl.when(s == first_total)
        def _():
            for copy in loads_adam:
                copy.wait()

        c2 = s - first_total - OUT_LAG * (mid_depth - depth)

        @pl.when(active(c2))
        def _():
            @pl.when(is_mid)
            def _():
                for p in range(pieces):
                    inward(c2, p, r2, back_r).wait_recv()
                    total = sb[c2, p].astype(jnp.float32) + r2[c2, p].astype(jnp.float32)
                    gt[c2, p] = total.astype(jnp.bfloat16)

                    @pl.when(depth > 0)
                    def _():
                        outward(c2, p).start()

            @pl.when(jnp.logical_not(is_mid))
            def _():
                for p in range(pieces):
                    outward(c2, p).wait_recv()

                    @pl.when(depth > 0)
                    def _():
                        outward(c2, p).start()

            @pl.when(c2 >= 2 * early)
            def _():
                update(row_block(c2), gt[c2].astype(jnp.float32))

        if early:

            @pl.when(s == to_other_at)
            def _():
                to_other().start()

            @pl.when(s == early_at)
            def _():
                to_other().wait_recv()
                update(row_block(0), gt[0].astype(jnp.float32) + other[...].astype(jnp.float32))

        def attend_next(part, none):
            attend(part)
            return none

        lax.fori_loop(parts_done(s - 1), parts_done(s), attend_next, 0)

        if early:

            @pl.when(s == 1)
            def _():
                cot_rest()

        return carry

    slots = max(n_z + last_total, max(MID_ATT_SLOTS + END_ATT_SLOTS) + 1, early_at + 1 if early else 0)
    lax.fori_loop(0, slots, slot, 0)

    def out_copy(k):
        peer = lax.rem(me + k, n_ft)
        return pltpu.make_async_remote_copy(
            src_ref=ps.at[k], dst_ref=pr.at[t * n_f + f], send_sem=pr_s.at[0], recv_sem=pr_r.at[0],
            device_id={"fsdp": peer // n_t, "tensor": peer % n_t}, device_id_type=MESH,
        )

    ps_all = acc.reshape(STEPS, acc.shape[0] // STEPS, width)
    for k in range(1, n_ft):
        peer = lax.rem(me + k, n_ft)
        take = pl.ds(pl.multiple_of(peer * row_dev, row_dev), row_dev)
        ps[k] = ps_all[:, take, :].reshape(STEPS * row_dev, width).astype(jnp.bfloat16)
        out_copy(k).start()
    take = pl.ds(pl.multiple_of(me * row_dev, row_dev), row_dev)
    pr[t * n_f + f] = ps_all[:, take, :].reshape(STEPS * row_dev, width).astype(jnp.bfloat16)
    for k in range(1, n_f):
        cot_copy(k).wait_send()
    arrived(tok.at[:, pl.ds(0, 1)], tok_s.at[0])
    arrived(tok.at[pl.ds(2 * early, n_z - 2 * early), pl.ds(2, n_f - 2)], tok_s.at[1])
    if early:
        to_other().wait_send()
    arrived(hid.at[pl.ds(0, per_t * (n_t - 1))], hid_s.at[0])
    arrived(sb, in_s.at[0])

    @pl.when(depth > 0)
    def _():
        arrived(gt, out_s.at[0])

    arrived(pr.at[pl.ds(0, n_ft - 1)], pr_r.at[0])
    fresh_parts = []
    for tt in range(n_t):
        total = pr[tt * n_f].astype(jnp.float32)
        for ff in range(1, n_f):
            total = total + pr[tt * n_f + ff].astype(jnp.float32)
        fresh_parts.append(total.astype(jnp.bfloat16))
    fresh[...] = jnp.concatenate(fresh_parts, axis=1)

    arrived(ps.at[pl.ds(0, n_ft - 1)], pr_s.at[0])


def finish_kernel(w_v, m1_v, m2_v, oc, pf, fresh, w_o, m1_o, m2_o, att_o, att_v, sems):
    copies = []
    for a, o, cuts in ((m1_v, m1_o, 4), (m2_v, m2_o, 4), (w_v, w_o, 2)):
        rows = a.shape[0] // cuts
        for j in range(cuts):
            span = pl.ds(j * rows, rows)
            copies.append(pltpu.make_async_copy(a.at[span], o.at[span], sems.at[len(copies)]))
            copies[-1].start()
    heads_part = KV_HEADS * GROUP_HEADS // ATT_PARTS
    steps, row_dev = att_v.shape[:2]
    block = steps * row_dev
    for part in range(ATT_PARTS):
        h = part * heads_part // GROUP_HEADS
        res = oc[part] + jnp.dot(
            pf[part], fresh[:, h * HEAD_DIM : (h + 1) * HEAD_DIM], preferred_element_type=jnp.float32
        )
        for j in range(heads_part):
            at = (part * heads_part + j) * HEAD_DIM
            att_v[:, :, at : at + HEAD_DIM] = (
                res[j * block : (j + 1) * block].reshape(steps, row_dev, HEAD_DIM).astype(jnp.bfloat16)
            )
        cols = pl.ds(part * heads_part * HEAD_DIM, heads_part * HEAD_DIM)
        copies.append(
            pltpu.make_async_copy(att_v.at[:, :, cols], att_o.at[:, :, cols], sems.at[len(copies)])
        )
        copies[-1].start()
    for copy in copies:
        copy.wait()


def finish(att_shape, w, m1, m2, *rest):
    spec = pl.BlockSpec(memory_space=pl.ANY)
    outs = [jax.ShapeDtypeStruct(a.shape, a.dtype) for a in (w, m1, m2)]
    outs.append(jax.ShapeDtypeStruct(att_shape, jnp.bfloat16))
    held = [pltpu.with_memory_space_constraint(a, pltpu.VMEM) for a in (w, m1, m2) + rest]
    return pl.pallas_call(
        finish_kernel,
        out_shape=tuple(outs),
        in_specs=[pl.BlockSpec(memory_space=pltpu.VMEM)] * len(held),
        out_specs=(spec,) * 4,
        scratch_shapes=[pltpu.VMEM(att_shape, jnp.bfloat16), pltpu.SemaphoreType.DMA((10 + ATT_PARTS,))],
        compiler_params=pltpu.CompilerParams(vmem_limit_bytes=16 * 1024 * 1024),
        name="finish",
    )(*held)


def per_device(
    n_g, n_f, n_t,
    tokens, cotangent, weight, moment_one, moment_two, hidden, queries, new_keys,
    key_cache, value_cache, lengths,
):
    n_ft = n_f * n_t
    rows, width = weight.shape
    n_c = max(CHUNKS, n_t)
    rows_c = rows // n_c
    row_dev, cache, kvw = key_cache.shape
    tok_rows = tokens.shape[0]
    early = 1 if n_f == 4 else 0
    n_z = n_c + early
    piece_shape = (n_z, PIECES, rows_c // PIECES, width)
    acc_rows = hidden.shape[0] * hidden.shape[1]
    n_q = KV_HEADS * GROUP_HEADS // ATT_PARTS * STEPS * row_dev
    bf16, f32 = jnp.bfloat16, jnp.float32
    dma = pltpu.SemaphoreType.DMA
    anywhere = pl.BlockSpec(memory_space=pl.ANY)
    scratch = [
        pltpu.VMEM((n_z, n_f, tok_rows, rows_c), bf16),
        pltpu.VMEM((n_f, tok_rows, width), bf16),
        pltpu.VMEM((n_c,) + hidden.shape[:2] + (rows_c,), bf16),
        pltpu.VMEM(piece_shape, f32),
        pltpu.VMEM(piece_shape, bf16),
        pltpu.VMEM(piece_shape, bf16),
        pltpu.VMEM(piece_shape, bf16),
        pltpu.VMEM(piece_shape, bf16),
        pltpu.VMEM(piece_shape[1:], bf16),
        pltpu.VMEM(queries.shape, bf16),
        pltpu.VMEM(new_keys.shape, bf16),
        pltpu.VMEM(key_cache.shape, bf16),
        pltpu.VMEM(value_cache.shape, bf16),
        pltpu.VMEM((acc_rows, width), f32),
        pltpu.VMEM((n_ft, STEPS * row_dev, width), bf16),
        pltpu.VMEM((n_ft, STEPS * row_dev, width), bf16),
        dma((2,)), dma((n_z,)),
        dma((n_f,)), dma((n_f,)),
        dma((1,)), dma((n_c,)),
        dma((1,)), dma((1,)), dma((n_z, PIECES)), dma((n_z, PIECES)), dma((1,)), dma((1,)),
        dma((1,)), dma((1,)), dma((8,)),
    ]
    held = pl.pallas_call(
        functools.partial(kernel, n_g, n_f, n_t, n_c, early),
        out_shape=(
            pltpu.VMEM(weight.shape, bf16),
            pltpu.VMEM(weight.shape, f32),
            pltpu.VMEM(weight.shape, f32),
            pltpu.VMEM((ATT_PARTS, n_q, HEAD_DIM), f32),
            pltpu.VMEM((ATT_PARTS, n_q, STEPS * row_dev), bf16),
            pltpu.VMEM((STEPS * row_dev, n_t * width), bf16),
        ),
        in_specs=[pl.BlockSpec(memory_space=pltpu.SMEM)] + [anywhere] * 10,
        out_specs=(pl.BlockSpec(memory_space=pltpu.VMEM),) * 6,
        scratch_shapes=scratch,
        compiler_params=pltpu.CompilerParams(
            collective_id=0, has_side_effects=True, vmem_limit_bytes=48 * 1024 * 1024
        ),
        name="step",
    )(
        lengths, tokens, cotangent, weight, moment_one, moment_two, hidden, queries, new_keys,
        key_cache, value_cache,
    )
    return finish(queries.shape, *held)


def solution(mesh):
    in_specs = (
        P(("group", "fsdp"), None),
        P(("group", "fsdp"), "tensor"),
        P("fsdp", "tensor"),
        P("fsdp", "tensor"),
        P("fsdp", "tensor"),
        P(None, "group", ("fsdp", "tensor")),
        P(None, ("group", "fsdp", "tensor"), None),
        P(None, ("group", "fsdp", "tensor"), None),
        P(("group", "fsdp", "tensor"), None, None),
        P(("group", "fsdp", "tensor"), None, None),
        P(("group", "fsdp", "tensor")),
    )
    out_specs = (
        P("fsdp", "tensor"),
        P("fsdp", "tensor"),
        P("fsdp", "tensor"),
        P(None, ("group", "fsdp", "tensor"), None),
    )
    sizes = (mesh.shape["group"], mesh.shape["fsdp"], mesh.shape["tensor"])
    return jax.shard_map(
        functools.partial(per_device, *sizes),
        mesh=mesh, in_specs=in_specs, out_specs=out_specs, check_vma=False,
    )
```

```python
import functools

import jax
import jax.numpy as jnp
from jax import lax
from jax.experimental import pallas as pl
from jax.experimental.pallas import tpu as pltpu
from jax.sharding import PartitionSpec as P

HEAD_DIM = 128
GROUP_HEADS = 8
KV_HEADS = 4
STEPS = 4
ADAM_STEP = 10

CHUNKS = 16
PIECES = 2
IN_LAG = 1
MID_LAG = 2
OUT_LAG = 4
ATT_PARTS = 8
MID_ATT_SLOTS = (0, 0, 0, 0, 2, 3, 4, 5)
END_ATT_SLOTS = (1, 1, 2, 3, 4, 5, 6, 7)
AHEAD = 4
EARLY_WAIT = 4

learn_rate = 0.001
beta_one = 0.9
beta_two = 0.95
epsilon = 1e-08
decay_rate = 0.1
masked_score = -1e30

MESH = pl.DeviceIdType.MESH


def adamw(gradient, weight, moment_one, moment_two):
    first_new = beta_one * moment_one + (1.0 - beta_one) * gradient
    second_new = beta_two * moment_two + (1.0 - beta_two) * gradient * gradient
    first_hat = first_new * (1.0 / (1.0 - beta_one**ADAM_STEP))
    second_hat = second_new * (1.0 / (1.0 - beta_two**ADAM_STEP))
    stepped = weight.astype(jnp.float32) * (
        1.0 - learn_rate * decay_rate
    ) - learn_rate * first_hat / (jnp.sqrt(second_hat) + epsilon)
    return stepped.astype(jnp.bfloat16), first_new, second_new


def kernel(
    n_g, n_f, n_t, n_c, early,
    lens, tokens, cot, weight, mom1, mom2, hidden, queries, new_keys, kcache, vcache,
    w_v, m1_v, m2_v, oc, pf, fresh,
    tok, cots, hid, own, sb, r1, r2, gt, other, q_v, nk_v, kc_v, vc_v,
    acc, ps, pr,
    tok_s, tok_r, cot_s, cot_r, hid_s, hid_r, in_s, out_s, r1_r, back_r, other_s, other_r,
    pr_s, pr_r, loc,
):
    g = lax.axis_index("group")
    f = lax.axis_index("fsdp")
    t = lax.axis_index("tensor")
    n_ft = n_f * n_t
    me = f * n_t + t
    rows_c = tok.shape[3]
    rows = n_c * rows_c
    per_t = n_c // n_t
    n_z = n_c + early
    row_dev = kc_v.shape[0]
    cache = kc_v.shape[1]
    width = cot.shape[1]

    mid_l, mid_r = n_g // 2 - 1, n_g // 2
    on_left = g <= mid_l
    toward = jnp.where(on_left, 1, -1)
    depth = jnp.where(on_left, g, n_g - 1 - g)
    mid_depth = jnp.where(on_left, mid_l, n_g - 1 - mid_r)
    is_mid = depth == mid_depth
    max_depth = max(mid_l, n_g - 1 - mid_r)

    barrier = pltpu.get_barrier_semaphore()
    for k in range(1, n_ft):
        peer = lax.rem(me + k, n_ft)
        pl.semaphore_signal(
            barrier, inc=1, device_id={"fsdp": peer // n_t, "tensor": peer % n_t}, device_id_type=MESH
        )

    def tell(to):
        pl.semaphore_signal(
            barrier, inc=1, device_id={"group": lax.rem(g + to + n_g, n_g)}, device_id_type=MESH
        )

    @pl.when(is_mid)
    def _():
        tell(toward)

    def local(src, dst, sem):
        copy = pltpu.make_async_copy(src, dst, sem)
        copy.start()
        return copy

    def row_block(c):
        return lax.rem(jnp.maximum(c - early, 0) + t * per_t, n_c)

    def across(i):
        return (i // 2 * 2 + 2) % n_f + i % 2

    def tok_column(c, to):
        owner = jnp.where(c == 1, across(to), to) if early else to
        return pl.multiple_of(owner * rows + row_block(c) * rows_c, rows_c)

    def tok_local(c):
        return pltpu.make_async_copy(
            tokens.at[:, pl.ds(tok_column(c, f), rows_c)], tok.at[c, 0], tok_r.at[c]
        )

    def hid_local(j):
        return pltpu.make_async_copy(
            hidden.at[:, :, pl.ds(j * rows_c, rows_c)], hid.at[t * per_t + j], hid_r.at[t * per_t + j]
        )

    cot_l = local(cot, cots.at[0], loc.at[0])
    loads_att = [
        local(queries, q_v, loc.at[1]),
        local(new_keys, nk_v, loc.at[2]),
        local(kcache, kc_v, loc.at[3]),
        local(vcache, vc_v, loc.at[4]),
    ]
    for c in range(AHEAD):
        tok_local(c).start()

    @pl.when((depth == 0) & jnp.logical_not(is_mid))
    def _():
        pl.semaphore_wait(barrier, n_ft - 1)

    @pl.when((depth == 0) & is_mid)
    def _():
        pl.semaphore_wait(barrier, n_ft)

    @pl.when((depth > 0) & jnp.logical_not(is_mid))
    def _():
        pl.semaphore_wait(barrier, n_ft)
        tell(-toward)

    @pl.when((depth > 0) & is_mid)
    def _():
        pl.semaphore_wait(barrier, n_ft + 1)
        tell(-toward)

    @pl.when(jnp.logical_not(is_mid))
    def _():
        tell(toward)

    def fsdp_peer(k):
        return (f // 2 * 2 + k // 2 * 2) % n_f + (f % 2 + k % 2) % 2

    def cot_copy(k):
        return pltpu.make_async_remote_copy(
            src_ref=cots.at[k - 1] if k % 2 and k > 1 else cot, dst_ref=cots.at[k],
            send_sem=cot_s.at[k], recv_sem=cot_r.at[k],
            device_id={"fsdp": fsdp_peer(1 if k % 2 else k)}, device_id_type=MESH,
        )

    def tok_copy(c, k):
        peer = fsdp_peer(k)
        return pltpu.make_async_remote_copy(
            src_ref=tokens.at[:, pl.ds(tok_column(c, peer), rows_c)], dst_ref=tok.at[c, k],
            send_sem=tok_s.at[min(k, 2) - 1], recv_sem=tok_r.at[c],
            device_id={"fsdp": peer}, device_id_type=MESH,
        )

    def hid_copy(j, k):
        return pltpu.make_async_remote_copy(
            src_ref=hidden.at[:, :, pl.ds(j * rows_c, rows_c)], dst_ref=hid.at[t * per_t + j],
            send_sem=hid_s.at[0], recv_sem=hid_r.at[t * per_t + j],
            device_id={"tensor": lax.rem(t + k, n_t)}, device_id_type=MESH,
        )

    def arrived(ref, sem):
        pltpu.make_async_copy(ref, ref, sem).wait()

    def send_tokens(c):
        @pl.when((early == 0) | (c >= 2))
        def _():
            for k in range(n_f - 1, 1, -1):
                tok_copy(c, k).start()

        tok_copy(c, 1).start()

    for k in range(2, n_f, 2):
        cot_copy(k).start()
    cot_copy(1).start()
    for c in range(AHEAD):
        send_tokens(c)

    loads_adam = [
        local(weight, w_v, loc.at[5]),
        local(mom1, m1_v, loc.at[6]),
        local(mom2, m2_v, loc.at[7]),
    ]
    for copy in loads_att:
        copy.wait()

    heads_part = KV_HEADS * GROUP_HEADS // ATT_PARTS

    def attend(part):
        h = part * heads_part // GROUP_HEADS
        qs = [
            q_v[:, :, pl.ds(pl.multiple_of((part * heads_part + j) * HEAD_DIM, HEAD_DIM), HEAD_DIM)]
            .reshape(STEPS * row_dev, HEAD_DIM)
            for j in range(heads_part)
        ]
        q = jnp.concatenate(qs, axis=0)
        cols = pl.ds(pl.multiple_of(h * HEAD_DIM, HEAD_DIM), HEAD_DIM)
        kk = kc_v[:, :, cols].reshape(row_dev * cache, HEAD_DIM)
        fk = nk_v[:, :, cols].reshape(STEPS * row_dev, HEAD_DIM)
        vv = vc_v[:, :, cols].reshape(row_dev * cache, HEAD_DIM)
        contract = (((1,), (1,)), ((), ()))
        scale = HEAD_DIM ** (-0.5)
        s_c = lax.dot_general(q, kk, contract, preferred_element_type=jnp.float32) * scale
        s_f = lax.dot_general(q, fk, contract, preferred_element_type=jnp.float32) * scale
        n_q = q.shape[0]
        col_c = lax.broadcasted_iota(jnp.int32, (1, row_dev * cache), 1)
        col_row = col_c // cache
        limit = jnp.zeros_like(col_c)
        for r in range(row_dev):
            limit = jnp.where(col_row == r, lens[r], limit)
        col_row = jnp.where(col_c % cache < limit, col_row, -1)
        q_id = lax.broadcasted_iota(jnp.int32, (n_q, 1), 0)
        q_row = q_id % row_dev
        q_step = (q_id // row_dev) % STEPS
        col_f = lax.broadcasted_iota(jnp.int32, (1, STEPS * row_dev), 1)
        ok_c = q_row == col_row
        ok_f = (q_row == col_f % row_dev) & (col_f // row_dev <= q_step)
        s_c = jnp.where(ok_c, s_c, masked_score)
        s_f = jnp.where(ok_f, s_f, masked_score)
        highest = jnp.maximum(
            jnp.max(s_c, axis=-1, keepdims=True), jnp.max(s_f, axis=-1, keepdims=True)
        )
        e_c = jnp.exp(s_c - highest)
        e_f = jnp.exp(s_f - highest)
        den = jnp.sum(e_c, axis=-1, keepdims=True) + jnp.sum(e_f, axis=-1, keepdims=True)
        p_c = (e_c / den).astype(jnp.bfloat16)
        pf[part] = (e_f / den).astype(jnp.bfloat16)
        oc[part] = jnp.dot(p_c, vv, preferred_element_type=jnp.float32)

    acc[...] = jnp.zeros_like(acc)
    cot_l.wait()
    cot_copy(1).wait_recv()

    def cot_rest():
        for k in range(2, n_f, 2):
            cot_copy(k).wait_recv()
            cot_copy(k + 1).start()

    def cot_ready():
        for k in range(3, n_f, 2):
            cot_copy(k).wait_recv()

    if not early:
        cot_rest()
        cot_ready()

    @pl.when(jnp.logical_not(is_mid))
    def _():
        pl.semaphore_wait(barrier, 1)

    def parts_done(s):
        mid = sum((s >= at).astype(jnp.int32) for at in MID_ATT_SLOTS)
        end = sum((s >= at).astype(jnp.int32) for at in END_ATT_SLOTS)
        return jnp.where(is_mid, mid, end)

    def inward(c, p, dst, recv):
        return pltpu.make_async_remote_copy(
            src_ref=sb.at[c, p], dst_ref=dst.at[c, p], send_sem=in_s.at[0], recv_sem=recv.at[c, p],
            device_id={"group": lax.rem(g + toward + n_g, n_g)}, device_id_type=MESH,
        )

    def outward(c, p):
        return pltpu.make_async_remote_copy(
            src_ref=gt.at[c, p], dst_ref=gt.at[c, p], send_sem=out_s.at[0], recv_sem=back_r.at[c, p],
            device_id={"group": lax.rem(g - toward + n_g, n_g)}, device_id_type=MESH,
        )

    def send_inward(c, p, part):
        sb[c, p] = part.astype(jnp.bfloat16)

        @pl.when(is_mid)
        def _():
            inward(c, p, r2, back_r).start()

        @pl.when(jnp.logical_not(is_mid))
        def _():
            inward(c, p, r1, r1_r).start()

    def active(c):
        return (c >= 0) & (c < n_z)

    def to_other():
        return pltpu.make_async_remote_copy(
            src_ref=gt.at[1], dst_ref=other, send_sem=other_s.at[0], recv_sem=other_r.at[0],
            device_id={"fsdp": fsdp_peer(2)}, device_id_type=MESH,
        )

    pieces, piece = sb.shape[1:3]
    first_total = IN_LAG * max_depth + MID_LAG

    def gradient(block, cot_block):
        k = block.shape[0] * block.shape[1]
        return lax.dot_general(
            block.reshape(k, rows_c), cot_block.reshape(k, width), (((0,), (0,)), ((), ())),
            preferred_element_type=jnp.float32,
        )

    def place(s, grad):
        @pl.when(depth == 0)
        def _():
            for p in range(pieces):
                send_inward(s, p, grad[p * piece : (p + 1) * piece])

        @pl.when(depth > 0)
        def _():
            for p in range(pieces):
                own[s, p] = grad[p * piece : (p + 1) * piece]

    def update(b, grad):
        arrived(hid.at[b], hid_r.at[b])
        span = pl.ds(pl.multiple_of(b * rows_c, rows_c), rows_c)
        w_new, m1_new, m2_new = adamw(
            grad.reshape(rows_c, width), w_v[span], m1_v[span], m2_v[span]
        )
        w_v[span] = w_new
        m1_v[span] = m1_new
        m2_v[span] = m2_new
        lhs = hid[b].reshape(acc.shape[0], rows_c)
        acc[...] += jnp.dot(lhs, w_new, preferred_element_type=jnp.float32)

    last_total = first_total + OUT_LAG * max_depth
    to_other_at = max(n_z - 1, last_total + 2)
    early_at = to_other_at + EARLY_WAIT

    def slot(s, carry):
        @pl.when(s < n_z - AHEAD)
        def _():
            tok_local(s + AHEAD).start()
            send_tokens(s + AHEAD)

        @pl.when(s < per_t)
        def _():
            for k in range(1, n_t):
                hid_copy(s, k).start()
            hid_local(s).start()

        if early:

            @pl.when(s < 2)
            def _():
                arrived(tok.at[s, pl.ds(0, 2)], tok_r.at[s])
                place(s, gradient(tok[s, 0:2], cots[0:2]))

            @pl.when(s == 2)
            def _():
                cot_ready()

        @pl.when((s >= 2 * early) & (s < n_z))
        def _():
            arrived(tok.at[s], tok_r.at[s])
            place(s, gradient(tok[s], cots[...]))

        c1 = s - IN_LAG * depth

        @pl.when((depth > 0) & active(c1))
        def _():
            for p in range(pieces):
                inward(c1, p, r1, r1_r).wait_recv()
                send_inward(c1, p, own[c1, p] + r1[c1, p].astype(jnp.float32))

        @pl.when(s == first_total)
        def _():
            for copy in loads_adam:
                copy.wait()

        c2 = s - first_total - OUT_LAG * (mid_depth - depth)
        c3 = c2 - 1

        @pl.when((c3 >= 2 * early) & (c3 < n_z))
        def _():
            update(row_block(c3), gt[c3].astype(jnp.float32))

        if early:

            @pl.when(s == to_other_at)
            def _():
                to_other().start()

            @pl.when(s == early_at)
            def _():
                to_other().wait_recv()
                update(row_block(0), gt[0].astype(jnp.float32) + other[...].astype(jnp.float32))

        def attend_next(part, none):
            attend(part)
            return none

        lax.fori_loop(parts_done(s - 1), parts_done(s), attend_next, 0)

        if early:

            @pl.when(s == 1)
            def _():
                cot_rest()

        @pl.when(active(c2))
        def _():
            @pl.when(is_mid)
            def _():
                for p in range(pieces):
                    inward(c2, p, r2, back_r).wait_recv()
                    total = sb[c2, p].astype(jnp.float32) + r2[c2, p].astype(jnp.float32)
                    gt[c2, p] = total.astype(jnp.bfloat16)

                    @pl.when(depth > 0)
                    def _():
                        outward(c2, p).start()

            @pl.when(jnp.logical_not(is_mid))
            def _():
                for p in range(pieces):
                    outward(c2, p).wait_recv()

                    @pl.when(depth > 0)
                    def _():
                        outward(c2, p).start()

        return carry

    slots = max(n_z + last_total + 1, max(MID_ATT_SLOTS + END_ATT_SLOTS) + 1, early_at + 1 if early else 0)
    lax.fori_loop(0, slots, slot, 0)

    def out_copy(k):
        peer = lax.rem(me + k, n_ft)
        return pltpu.make_async_remote_copy(
            src_ref=ps.at[k], dst_ref=pr.at[t * n_f + f], send_sem=pr_s.at[0], recv_sem=pr_r.at[0],
            device_id={"fsdp": peer // n_t, "tensor": peer % n_t}, device_id_type=MESH,
        )

    ps_all = acc.reshape(STEPS, acc.shape[0] // STEPS, width)
    for k in range(1, n_ft):
        peer = lax.rem(me + k, n_ft)
        take = pl.ds(pl.multiple_of(peer * row_dev, row_dev), row_dev)
        ps[k] = ps_all[:, take, :].reshape(STEPS * row_dev, width).astype(jnp.bfloat16)
        out_copy(k).start()
    take = pl.ds(pl.multiple_of(me * row_dev, row_dev), row_dev)
    pr[t * n_f + f] = ps_all[:, take, :].reshape(STEPS * row_dev, width).astype(jnp.bfloat16)
    for k in range(1, n_f):
        cot_copy(k).wait_send()
    arrived(tok.at[:, pl.ds(0, 1)], tok_s.at[0])
    arrived(tok.at[pl.ds(2 * early, n_z - 2 * early), pl.ds(2, n_f - 2)], tok_s.at[1])
    if early:
        to_other().wait_send()
    arrived(hid.at[pl.ds(0, per_t * (n_t - 1))], hid_s.at[0])
    arrived(sb, in_s.at[0])

    @pl.when(depth > 0)
    def _():
        arrived(gt, out_s.at[0])

    arrived(pr.at[pl.ds(0, n_ft - 1)], pr_r.at[0])
    fresh_parts = []
    for tt in range(n_t):
        total = pr[tt * n_f].astype(jnp.float32)
        for ff in range(1, n_f):
            total = total + pr[tt * n_f + ff].astype(jnp.float32)
        fresh_parts.append(total.astype(jnp.bfloat16))
    fresh[...] = jnp.concatenate(fresh_parts, axis=1)

    arrived(ps.at[pl.ds(0, n_ft - 1)], pr_s.at[0])


def finish_kernel(w_v, m1_v, m2_v, oc, pf, fresh, w_o, m1_o, m2_o, att_o, att_v, sems):
    copies = []
    for a, o, cuts in ((m1_v, m1_o, 4), (m2_v, m2_o, 4), (w_v, w_o, 2)):
        rows = a.shape[0] // cuts
        for j in range(cuts):
            span = pl.ds(j * rows, rows)
            copies.append(pltpu.make_async_copy(a.at[span], o.at[span], sems.at[len(copies)]))
            copies[-1].start()
    heads_part = KV_HEADS * GROUP_HEADS // ATT_PARTS
    steps, row_dev = att_v.shape[:2]
    block = steps * row_dev
    for part in range(ATT_PARTS):
        h = part * heads_part // GROUP_HEADS
        res = oc[part] + jnp.dot(
            pf[part], fresh[:, h * HEAD_DIM : (h + 1) * HEAD_DIM], preferred_element_type=jnp.float32
        )
        for j in range(heads_part):
            at = (part * heads_part + j) * HEAD_DIM
            att_v[:, :, at : at + HEAD_DIM] = (
                res[j * block : (j + 1) * block].reshape(steps, row_dev, HEAD_DIM).astype(jnp.bfloat16)
            )
        cols = pl.ds(part * heads_part * HEAD_DIM, heads_part * HEAD_DIM)
        copies.append(
            pltpu.make_async_copy(att_v.at[:, :, cols], att_o.at[:, :, cols], sems.at[len(copies)])
        )
        copies[-1].start()
    for copy in copies:
        copy.wait()


def finish(att_shape, w, m1, m2, *rest):
    spec = pl.BlockSpec(memory_space=pl.ANY)
    outs = [jax.ShapeDtypeStruct(a.shape, a.dtype) for a in (w, m1, m2)]
    outs.append(jax.ShapeDtypeStruct(att_shape, jnp.bfloat16))
    held = [pltpu.with_memory_space_constraint(a, pltpu.VMEM) for a in (w, m1, m2) + rest]
    return pl.pallas_call(
        finish_kernel,
        out_shape=tuple(outs),
        in_specs=[pl.BlockSpec(memory_space=pltpu.VMEM)] * len(held),
        out_specs=(spec,) * 4,
        scratch_shapes=[pltpu.VMEM(att_shape, jnp.bfloat16), pltpu.SemaphoreType.DMA((10 + ATT_PARTS,))],
        compiler_params=pltpu.CompilerParams(vmem_limit_bytes=16 * 1024 * 1024),
        name="finish",
    )(*held)


def per_device(
    n_g, n_f, n_t,
    tokens, cotangent, weight, moment_one, moment_two, hidden, queries, new_keys,
    key_cache, value_cache, lengths,
):
    n_ft = n_f * n_t
    rows, width = weight.shape
    n_c = max(CHUNKS, n_t)
    rows_c = rows // n_c
    row_dev, cache, kvw = key_cache.shape
    tok_rows = tokens.shape[0]
    early = 1 if n_f == 4 else 0
    n_z = n_c + early
    piece_shape = (n_z, PIECES, rows_c // PIECES, width)
    acc_rows = hidden.shape[0] * hidden.shape[1]
    n_q = KV_HEADS * GROUP_HEADS // ATT_PARTS * STEPS * row_dev
    bf16, f32 = jnp.bfloat16, jnp.float32
    dma = pltpu.SemaphoreType.DMA
    anywhere = pl.BlockSpec(memory_space=pl.ANY)
    scratch = [
        pltpu.VMEM((n_z, n_f, tok_rows, rows_c), bf16),
        pltpu.VMEM((n_f, tok_rows, width), bf16),
        pltpu.VMEM((n_c,) + hidden.shape[:2] + (rows_c,), bf16),
        pltpu.VMEM(piece_shape, f32),
        pltpu.VMEM(piece_shape, bf16),
        pltpu.VMEM(piece_shape, bf16),
        pltpu.VMEM(piece_shape, bf16),
        pltpu.VMEM(piece_shape, bf16),
        pltpu.VMEM(piece_shape[1:], bf16),
        pltpu.VMEM(queries.shape, bf16),
        pltpu.VMEM(new_keys.shape, bf16),
        pltpu.VMEM(key_cache.shape, bf16),
        pltpu.VMEM(value_cache.shape, bf16),
        pltpu.VMEM((acc_rows, width), f32),
        pltpu.VMEM((n_ft, STEPS * row_dev, width), bf16),
        pltpu.VMEM((n_ft, STEPS * row_dev, width), bf16),
        dma((2,)), dma((n_z,)),
        dma((n_f,)), dma((n_f,)),
        dma((1,)), dma((n_c,)),
        dma((1,)), dma((1,)), dma((n_z, PIECES)), dma((n_z, PIECES)), dma((1,)), dma((1,)),
        dma((1,)), dma((1,)), dma((8,)),
    ]
    held = pl.pallas_call(
        functools.partial(kernel, n_g, n_f, n_t, n_c, early),
        out_shape=(
            pltpu.VMEM(weight.shape, bf16),
            pltpu.VMEM(weight.shape, f32),
            pltpu.VMEM(weight.shape, f32),
            pltpu.VMEM((ATT_PARTS, n_q, HEAD_DIM), f32),
            pltpu.VMEM((ATT_PARTS, n_q, STEPS * row_dev), bf16),
            pltpu.VMEM((STEPS * row_dev, n_t * width), bf16),
        ),
        in_specs=[pl.BlockSpec(memory_space=pltpu.SMEM)] + [anywhere] * 10,
        out_specs=(pl.BlockSpec(memory_space=pltpu.VMEM),) * 6,
        scratch_shapes=scratch,
        compiler_params=pltpu.CompilerParams(
            collective_id=0, has_side_effects=True, vmem_limit_bytes=48 * 1024 * 1024
        ),
        name="step",
    )(
        lengths, tokens, cotangent, weight, moment_one, moment_two, hidden, queries, new_keys,
        key_cache, value_cache,
    )
    return finish(queries.shape, *held)


def solution(mesh):
    in_specs = (
        P(("group", "fsdp"), None),
        P(("group", "fsdp"), "tensor"),
        P("fsdp", "tensor"),
        P("fsdp", "tensor"),
        P("fsdp", "tensor"),
        P(None, "group", ("fsdp", "tensor")),
        P(None, ("group", "fsdp", "tensor"), None),
        P(None, ("group", "fsdp", "tensor"), None),
        P(("group", "fsdp", "tensor"), None, None),
        P(("group", "fsdp", "tensor"), None, None),
        P(("group", "fsdp", "tensor")),
    )
    out_specs = (
        P("fsdp", "tensor"),
        P("fsdp", "tensor"),
        P("fsdp", "tensor"),
        P(None, ("group", "fsdp", "tensor"), None),
    )
    sizes = (mesh.shape["group"], mesh.shape["fsdp"], mesh.shape["tensor"])
    return jax.shard_map(
        functools.partial(per_device, *sizes),
        mesh=mesh, in_specs=in_specs, out_specs=out_specs, check_vma=False,
    )
```

```python
import functools

import jax
import jax.numpy as jnp
from jax import lax
from jax.experimental import pallas as pl
from jax.experimental.pallas import tpu as pltpu
from jax.sharding import PartitionSpec as P

HEAD_DIM = 128
GROUP_HEADS = 8
KV_HEADS = 4
STEPS = 4
ADAM_STEP = 10

CHUNKS = 16
PIECES = 2
IN_LAG = 1
MID_LAG = 2
OUT_LAG = 4
ATT_PARTS = 8
MID_ATT_SLOTS = (0, 0, 0, 0, 2, 3, 4, 5)
END_ATT_SLOTS = (1, 1, 2, 3, 4, 5, 6, 7)
AHEAD = 4
EARLY_WAIT = 4

learn_rate = 0.001
beta_one = 0.9
beta_two = 0.95
epsilon = 1e-08
decay_rate = 0.1
masked_score = -1e30

MESH = pl.DeviceIdType.MESH


def adamw(gradient, weight, moment_one, moment_two):
    first_new = beta_one * moment_one + (1.0 - beta_one) * gradient
    second_new = beta_two * moment_two + (1.0 - beta_two) * gradient * gradient
    first_hat = first_new * (1.0 / (1.0 - beta_one**ADAM_STEP))
    second_hat = second_new * (1.0 / (1.0 - beta_two**ADAM_STEP))
    stepped = weight.astype(jnp.float32) * (
        1.0 - learn_rate * decay_rate
    ) - learn_rate * first_hat / (jnp.sqrt(second_hat) + epsilon)
    return stepped.astype(jnp.bfloat16), first_new, second_new


def kernel(
    n_g, n_f, n_t, n_c, early,
    lens, tokens, cot, weight, mom1, mom2, hidden, queries, new_keys, kcache, vcache,
    w_v, m1_v, m2_v, oc, pf, fresh,
    tok, cots, hid, own, sb, r1, r2, gt, other, q_v, nk_v, kc_v, vc_v,
    acc, ps, pr,
    tok_s, tok_r, cot_s, cot_r, hid_s, hid_r, in_s, out_s, r1_r, back_r, other_s, other_r,
    pr_s, pr_r, loc,
):
    g = lax.axis_index("group")
    f = lax.axis_index("fsdp")
    t = lax.axis_index("tensor")
    n_ft = n_f * n_t
    me = f * n_t + t
    rows_c = tok.shape[3]
    rows = n_c * rows_c
    per_t = n_c // n_t
    n_z = n_c + early
    row_dev = kc_v.shape[0]
    cache = kc_v.shape[1]
    width = cot.shape[1]

    mid_l, mid_r = n_g // 2 - 1, n_g // 2
    on_left = g <= mid_l
    toward = jnp.where(on_left, 1, -1)
    depth = jnp.where(on_left, g, n_g - 1 - g)
    mid_depth = jnp.where(on_left, mid_l, n_g - 1 - mid_r)
    is_mid = depth == mid_depth
    max_depth = max(mid_l, n_g - 1 - mid_r)

    barrier = pltpu.get_barrier_semaphore()
    for k in range(1, n_ft):
        peer = lax.rem(me + k, n_ft)
        pl.semaphore_signal(
            barrier, inc=1, device_id={"fsdp": peer // n_t, "tensor": peer % n_t}, device_id_type=MESH
        )

    def tell(to):
        pl.semaphore_signal(
            barrier, inc=1, device_id={"group": lax.rem(g + to + n_g, n_g)}, device_id_type=MESH
        )

    @pl.when(is_mid)
    def _():
        tell(toward)

    def local(src, dst, sem):
        copy = pltpu.make_async_copy(src, dst, sem)
        copy.start()
        return copy

    def row_block(c):
        return lax.rem(jnp.maximum(c - early, 0) + t * per_t, n_c)

    def across(i):
        return (i // 2 * 2 + 2) % n_f + i % 2

    def tok_column(c, to):
        owner = jnp.where(c == 1, across(to), to) if early else to
        return pl.multiple_of(owner * rows + row_block(c) * rows_c, rows_c)

    def tok_local(c):
        return pltpu.make_async_copy(
            tokens.at[:, pl.ds(tok_column(c, f), rows_c)], tok.at[c, 0], tok_r.at[c]
        )

    def hid_local(j):
        return pltpu.make_async_copy(
            hidden.at[:, :, pl.ds(j * rows_c, rows_c)], hid.at[t * per_t + j], hid_r.at[t * per_t + j]
        )

    cot_l = local(cot, cots.at[0], loc.at[0])
    loads_att = [
        local(queries, q_v, loc.at[1]),
        local(new_keys, nk_v, loc.at[2]),
        local(kcache, kc_v, loc.at[3]),
        local(vcache, vc_v, loc.at[4]),
    ]
    for c in range(AHEAD):
        tok_local(c).start()

    @pl.when((depth == 0) & jnp.logical_not(is_mid))
    def _():
        pl.semaphore_wait(barrier, n_ft - 1)

    @pl.when((depth == 0) & is_mid)
    def _():
        pl.semaphore_wait(barrier, n_ft)

    @pl.when((depth > 0) & jnp.logical_not(is_mid))
    def _():
        pl.semaphore_wait(barrier, n_ft)
        tell(-toward)

    @pl.when((depth > 0) & is_mid)
    def _():
        pl.semaphore_wait(barrier, n_ft + 1)
        tell(-toward)

    @pl.when(jnp.logical_not(is_mid))
    def _():
        tell(toward)

    def fsdp_peer(k):
        return (f // 2 * 2 + k // 2 * 2) % n_f + (f % 2 + k % 2) % 2

    def cot_copy(k):
        return pltpu.make_async_remote_copy(
            src_ref=cots.at[k - 1] if k % 2 and k > 1 else cot, dst_ref=cots.at[k],
            send_sem=cot_s.at[0], recv_sem=cot_r.at[k],
            device_id={"fsdp": fsdp_peer(1 if k % 2 else k)}, device_id_type=MESH,
        )

    def tok_copy(c, k):
        peer = fsdp_peer(k)
        return pltpu.make_async_remote_copy(
            src_ref=tokens.at[:, pl.ds(tok_column(c, peer), rows_c)], dst_ref=tok.at[c, k],
            send_sem=tok_s.at[min(k, 2) - 1], recv_sem=tok_r.at[c],
            device_id={"fsdp": peer}, device_id_type=MESH,
        )

    def hid_copy(j, k):
        return pltpu.make_async_remote_copy(
            src_ref=hidden.at[:, :, pl.ds(j * rows_c, rows_c)], dst_ref=hid.at[t * per_t + j],
            send_sem=hid_s.at[0], recv_sem=hid_r.at[t * per_t + j],
            device_id={"tensor": lax.rem(t + k, n_t)}, device_id_type=MESH,
        )

    def arrived(ref, sem):
        pltpu.make_async_copy(ref, ref, sem).wait()

    def send_tokens(c):
        @pl.when((early == 0) | (c >= 2))
        def _():
            for k in range(n_f - 1, 1, -1):
                tok_copy(c, k).start()

        tok_copy(c, 1).start()

    for k in range(2, n_f, 2):
        cot_copy(k).start()
    cot_copy(1).start()
    for c in range(AHEAD):
        send_tokens(c)

    loads_adam = [
        local(weight, w_v, loc.at[5]),
        local(mom1, m1_v, loc.at[6]),
        local(mom2, m2_v, loc.at[7]),
    ]
    for copy in loads_att:
        copy.wait()

    heads_part = KV_HEADS * GROUP_HEADS // ATT_PARTS

    def attend(part):
        h = part * heads_part // GROUP_HEADS
        qs = [
            q_v[:, :, pl.ds(pl.multiple_of((part * heads_part + j) * HEAD_DIM, HEAD_DIM), HEAD_DIM)]
            .reshape(STEPS * row_dev, HEAD_DIM)
            for j in range(heads_part)
        ]
        q = jnp.concatenate(qs, axis=0)
        cols = pl.ds(pl.multiple_of(h * HEAD_DIM, HEAD_DIM), HEAD_DIM)
        kk = kc_v[:, :, cols].reshape(row_dev * cache, HEAD_DIM)
        fk = nk_v[:, :, cols].reshape(STEPS * row_dev, HEAD_DIM)
        vv = vc_v[:, :, cols].reshape(row_dev * cache, HEAD_DIM)
        contract = (((1,), (1,)), ((), ()))
        scale = HEAD_DIM ** (-0.5)
        s_c = lax.dot_general(q, kk, contract, preferred_element_type=jnp.float32) * scale
        s_f = lax.dot_general(q, fk, contract, preferred_element_type=jnp.float32) * scale
        n_q = q.shape[0]
        col_c = lax.broadcasted_iota(jnp.int32, (1, row_dev * cache), 1)
        col_row = col_c // cache
        limit = jnp.zeros_like(col_c)
        for r in range(row_dev):
            limit = jnp.where(col_row == r, lens[r], limit)
        col_row = jnp.where(col_c % cache < limit, col_row, -1)
        q_id = lax.broadcasted_iota(jnp.int32, (n_q, 1), 0)
        q_row = q_id % row_dev
        q_step = (q_id // row_dev) % STEPS
        col_f = lax.broadcasted_iota(jnp.int32, (1, STEPS * row_dev), 1)
        ok_c = q_row == col_row
        ok_f = (q_row == col_f % row_dev) & (col_f // row_dev <= q_step)
        s_c = jnp.where(ok_c, s_c, masked_score)
        s_f = jnp.where(ok_f, s_f, masked_score)
        highest = jnp.maximum(
            jnp.max(s_c, axis=-1, keepdims=True), jnp.max(s_f, axis=-1, keepdims=True)
        )
        e_c = jnp.exp(s_c - highest)
        e_f = jnp.exp(s_f - highest)
        den = jnp.sum(e_c, axis=-1, keepdims=True) + jnp.sum(e_f, axis=-1, keepdims=True)
        p_c = (e_c / den).astype(jnp.bfloat16)
        pf[part] = (e_f / den).astype(jnp.bfloat16)
        oc[part] = jnp.dot(p_c, vv, preferred_element_type=jnp.float32)

    acc[...] = jnp.zeros_like(acc)
    cot_l.wait()
    cot_copy(1).wait_recv()

    def cot_rest():
        for k in range(2, n_f, 2):
            cot_copy(k).wait_recv()
            cot_copy(k + 1).start()

    def cot_ready():
        for k in range(3, n_f, 2):
            cot_copy(k).wait_recv()

    if not early:
        cot_rest()
        cot_ready()

    @pl.when(jnp.logical_not(is_mid))
    def _():
        pl.semaphore_wait(barrier, 1)

    def parts_done(s):
        mid = sum((s >= at).astype(jnp.int32) for at in MID_ATT_SLOTS)
        end = sum((s >= at).astype(jnp.int32) for at in END_ATT_SLOTS)
        return jnp.where(is_mid, mid, end)

    window = r1_r.shape[0]

    def inward(c, p, dst, recv):
        return pltpu.make_async_remote_copy(
            src_ref=sb.at[c, p], dst_ref=dst.at[c, p], send_sem=in_s.at[0], recv_sem=recv.at[lax.rem(c, window), p],
            device_id={"group": lax.rem(g + toward + n_g, n_g)}, device_id_type=MESH,
        )

    def outward(c, p):
        return pltpu.make_async_remote_copy(
            src_ref=gt.at[c, p], dst_ref=gt.at[c, p], send_sem=out_s.at[0], recv_sem=back_r.at[lax.rem(c, window), p],
            device_id={"group": lax.rem(g - toward + n_g, n_g)}, device_id_type=MESH,
        )

    def send_inward(c, p, part):
        sb[c, p] = part.astype(jnp.bfloat16)

        @pl.when(is_mid)
        def _():
            inward(c, p, r2, back_r).start()

        @pl.when(jnp.logical_not(is_mid))
        def _():
            inward(c, p, r1, r1_r).start()

    def active(c):
        return (c >= 0) & (c < n_z)

    def to_other():
        return pltpu.make_async_remote_copy(
            src_ref=gt.at[1], dst_ref=other, send_sem=other_s.at[0], recv_sem=other_r.at[0],
            device_id={"fsdp": fsdp_peer(2)}, device_id_type=MESH,
        )

    pieces, piece = sb.shape[1:3]
    first_total = IN_LAG * max_depth + MID_LAG

    def gradient(block, cot_block):
        k = block.shape[0] * block.shape[1]
        return lax.dot_general(
            block.reshape(k, rows_c), cot_block.reshape(k, width), (((0,), (0,)), ((), ())),
            preferred_element_type=jnp.float32,
        )

    def place(s, grad):
        @pl.when(depth == 0)
        def _():
            for p in range(pieces):
                send_inward(s, p, grad[p * piece : (p + 1) * piece])

        @pl.when(depth > 0)
        def _():
            for p in range(pieces):
                own[s, p] = grad[p * piece : (p + 1) * piece]

    def update(b, grad):
        arrived(hid.at[b], hid_r.at[b])
        span = pl.ds(pl.multiple_of(b * rows_c, rows_c), rows_c)
        w_new, m1_new, m2_new = adamw(
            grad.reshape(rows_c, width), w_v[span], m1_v[span], m2_v[span]
        )
        w_v[span] = w_new
        m1_v[span] = m1_new
        m2_v[span] = m2_new
        lhs = hid[b].reshape(acc.shape[0], rows_c)
        acc[...] += jnp.dot(lhs, w_new, preferred_element_type=jnp.float32)

    last_total = first_total + OUT_LAG * max_depth
    to_other_at = max(n_z - 1, last_total + 2)
    early_at = to_other_at + EARLY_WAIT

    def slot(s, carry):
        @pl.when(s < n_z - AHEAD)
        def _():
            tok_local(s + AHEAD).start()
            send_tokens(s + AHEAD)

        @pl.when(s < per_t)
        def _():
            for k in range(1, n_t):
                hid_copy(s, k).start()
            hid_local(s).start()

        if early:

            @pl.when(s < 2)
            def _():
                arrived(tok.at[s, pl.ds(0, 2)], tok_r.at[s])
                place(s, gradient(tok[s, 0:2], cots[0:2]))

            @pl.when(s == 2)
            def _():
                cot_ready()

        @pl.when((s >= 2 * early) & (s < n_z))
        def _():
            arrived(tok.at[s], tok_r.at[s])
            place(s, gradient(tok[s], cots[...]))

        c1 = s - IN_LAG * depth

        @pl.when((depth > 0) & active(c1))
        def _():
            for p in range(pieces):
                inward(c1, p, r1, r1_r).wait_recv()
                send_inward(c1, p, own[c1, p] + r1[c1, p].astype(jnp.float32))

        @pl.when(s == first_total)
        def _():
            for copy in loads_adam:
                copy.wait()

        c2 = s - first_total - OUT_LAG * (mid_depth - depth)
        c3 = c2 - 1

        @pl.when((c3 >= 2 * early) & (c3 < n_z))
        def _():
            update(row_block(c3), gt[c3].astype(jnp.float32))

        if early:

            @pl.when(s == to_other_at)
            def _():
                to_other().start()

            @pl.when(s == early_at)
            def _():
                to_other().wait_recv()
                update(row_block(0), gt[0].astype(jnp.float32) + other[...].astype(jnp.float32))

        def attend_next(part, none):
            attend(part)
            return none

        lax.fori_loop(parts_done(s - 1), parts_done(s), attend_next, 0)

        if early:

            @pl.when(s == 1)
            def _():
                cot_rest()

        @pl.when(active(c2))
        def _():
            @pl.when(is_mid)
            def _():
                for p in range(pieces):
                    inward(c2, p, r2, back_r).wait_recv()
                    total = sb[c2, p].astype(jnp.float32) + r2[c2, p].astype(jnp.float32)
                    gt[c2, p] = total.astype(jnp.bfloat16)

                    @pl.when(depth > 0)
                    def _():
                        outward(c2, p).start()

            @pl.when(jnp.logical_not(is_mid))
            def _():
                for p in range(pieces):
                    outward(c2, p).wait_recv()

                    @pl.when(depth > 0)
                    def _():
                        outward(c2, p).start()

        return carry

    slots = max(n_z + last_total + 1, max(MID_ATT_SLOTS + END_ATT_SLOTS) + 1, early_at + 1 if early else 0)
    lax.fori_loop(0, slots, slot, 0)

    def out_copy(k):
        peer = lax.rem(me + k, n_ft)
        return pltpu.make_async_remote_copy(
            src_ref=ps.at[k], dst_ref=pr.at[t * n_f + f], send_sem=pr_s.at[0], recv_sem=pr_r.at[0],
            device_id={"fsdp": peer // n_t, "tensor": peer % n_t}, device_id_type=MESH,
        )

    ps_all = acc.reshape(STEPS, acc.shape[0] // STEPS, width)
    for k in range(1, n_ft):
        peer = lax.rem(me + k, n_ft)
        take = pl.ds(pl.multiple_of(peer * row_dev, row_dev), row_dev)
        ps[k] = ps_all[:, take, :].reshape(STEPS * row_dev, width).astype(jnp.bfloat16)
        out_copy(k).start()
    take = pl.ds(pl.multiple_of(me * row_dev, row_dev), row_dev)
    pr[t * n_f + f] = ps_all[:, take, :].reshape(STEPS * row_dev, width).astype(jnp.bfloat16)
    arrived(cots.at[pl.ds(1, n_f - 1)], cot_s.at[0])
    arrived(tok.at[:, pl.ds(0, 1)], tok_s.at[0])
    arrived(tok.at[pl.ds(2 * early, n_z - 2 * early), pl.ds(2, n_f - 2)], tok_s.at[1])
    if early:
        to_other().wait_send()
    arrived(hid.at[pl.ds(0, per_t * (n_t - 1))], hid_s.at[0])
    arrived(sb, in_s.at[0])

    @pl.when(depth > 0)
    def _():
        arrived(gt, out_s.at[0])

    arrived(pr.at[pl.ds(0, n_ft - 1)], pr_r.at[0])
    fresh_parts = []
    for tt in range(n_t):
        total = pr[tt * n_f].astype(jnp.float32)
        for ff in range(1, n_f):
            total = total + pr[tt * n_f + ff].astype(jnp.float32)
        fresh_parts.append(total.astype(jnp.bfloat16))
    fresh[...] = jnp.concatenate(fresh_parts, axis=1)

    arrived(ps.at[pl.ds(0, n_ft - 1)], pr_s.at[0])


def finish_kernel(w_v, m1_v, m2_v, oc, pf, fresh, w_o, m1_o, m2_o, att_o, att_v, sems):
    copies = []
    for a, o, cuts in ((m1_v, m1_o, 4), (m2_v, m2_o, 4), (w_v, w_o, 2)):
        rows = a.shape[0] // cuts
        for j in range(cuts):
            span = pl.ds(j * rows, rows)
            copies.append(pltpu.make_async_copy(a.at[span], o.at[span], sems.at[len(copies)]))
            copies[-1].start()
    heads_part = KV_HEADS * GROUP_HEADS // ATT_PARTS
    steps, row_dev = att_v.shape[:2]
    block = steps * row_dev
    for part in range(ATT_PARTS):
        h = part * heads_part // GROUP_HEADS
        res = oc[part] + jnp.dot(
            pf[part], fresh[:, h * HEAD_DIM : (h + 1) * HEAD_DIM], preferred_element_type=jnp.float32
        )
        for j in range(heads_part):
            at = (part * heads_part + j) * HEAD_DIM
            att_v[:, :, at : at + HEAD_DIM] = (
                res[j * block : (j + 1) * block].reshape(steps, row_dev, HEAD_DIM).astype(jnp.bfloat16)
            )
        cols = pl.ds(part * heads_part * HEAD_DIM, heads_part * HEAD_DIM)
        copies.append(
            pltpu.make_async_copy(att_v.at[:, :, cols], att_o.at[:, :, cols], sems.at[len(copies)])
        )
        copies[-1].start()
    for copy in copies:
        copy.wait()


def finish(att_shape, w, m1, m2, *rest):
    spec = pl.BlockSpec(memory_space=pl.ANY)
    outs = [jax.ShapeDtypeStruct(a.shape, a.dtype) for a in (w, m1, m2)]
    outs.append(jax.ShapeDtypeStruct(att_shape, jnp.bfloat16))
    held = [pltpu.with_memory_space_constraint(a, pltpu.VMEM) for a in (w, m1, m2) + rest]
    return pl.pallas_call(
        finish_kernel,
        out_shape=tuple(outs),
        in_specs=[pl.BlockSpec(memory_space=pltpu.VMEM)] * len(held),
        out_specs=(spec,) * 4,
        scratch_shapes=[pltpu.VMEM(att_shape, jnp.bfloat16), pltpu.SemaphoreType.DMA((10 + ATT_PARTS,))],
        compiler_params=pltpu.CompilerParams(vmem_limit_bytes=16 * 1024 * 1024),
        name="finish",
    )(*held)


def per_device(
    n_g, n_f, n_t,
    tokens, cotangent, weight, moment_one, moment_two, hidden, queries, new_keys,
    key_cache, value_cache, lengths,
):
    n_ft = n_f * n_t
    rows, width = weight.shape
    n_c = max(CHUNKS, n_t)
    rows_c = rows // n_c
    row_dev, cache, kvw = key_cache.shape
    tok_rows = tokens.shape[0]
    early = 1 if n_f == 4 else 0
    n_z = n_c + early
    max_depth = max(n_g // 2 - 1, n_g - 1 - n_g // 2)
    window = min(n_z, IN_LAG * max_depth + MID_LAG + OUT_LAG * max_depth + 2)
    piece_shape = (n_z, PIECES, rows_c // PIECES, width)
    acc_rows = hidden.shape[0] * hidden.shape[1]
    n_q = KV_HEADS * GROUP_HEADS // ATT_PARTS * STEPS * row_dev
    bf16, f32 = jnp.bfloat16, jnp.float32
    dma = pltpu.SemaphoreType.DMA
    anywhere = pl.BlockSpec(memory_space=pl.ANY)
    scratch = [
        pltpu.VMEM((n_z, n_f, tok_rows, rows_c), bf16),
        pltpu.VMEM((n_f, tok_rows, width), bf16),
        pltpu.VMEM((n_c,) + hidden.shape[:2] + (rows_c,), bf16),
        pltpu.VMEM(piece_shape, f32),
        pltpu.VMEM(piece_shape, bf16),
        pltpu.VMEM(piece_shape, bf16),
        pltpu.VMEM(piece_shape, bf16),
        pltpu.VMEM(piece_shape, bf16),
        pltpu.VMEM(piece_shape[1:], bf16),
        pltpu.VMEM(queries.shape, bf16),
        pltpu.VMEM(new_keys.shape, bf16),
        pltpu.VMEM(key_cache.shape, bf16),
        pltpu.VMEM(value_cache.shape, bf16),
        pltpu.VMEM((acc_rows, width), f32),
        pltpu.VMEM((n_ft, STEPS * row_dev, width), bf16),
        pltpu.VMEM((n_ft, STEPS * row_dev, width), bf16),
        dma((2,)), dma((n_z,)),
        dma((1,)), dma((n_f,)),
        dma((1,)), dma((n_c,)),
        dma((1,)), dma((1,)), dma((window, PIECES)), dma((window, PIECES)), dma((1,)), dma((1,)),
        dma((1,)), dma((1,)), dma((8,)),
    ]
    held = pl.pallas_call(
        functools.partial(kernel, n_g, n_f, n_t, n_c, early),
        out_shape=(
            pltpu.VMEM(weight.shape, bf16),
            pltpu.VMEM(weight.shape, f32),
            pltpu.VMEM(weight.shape, f32),
            pltpu.VMEM((ATT_PARTS, n_q, HEAD_DIM), f32),
            pltpu.VMEM((ATT_PARTS, n_q, STEPS * row_dev), bf16),
            pltpu.VMEM((STEPS * row_dev, n_t * width), bf16),
        ),
        in_specs=[pl.BlockSpec(memory_space=pltpu.SMEM)] + [anywhere] * 10,
        out_specs=(pl.BlockSpec(memory_space=pltpu.VMEM),) * 6,
        scratch_shapes=scratch,
        compiler_params=pltpu.CompilerParams(
            collective_id=0, has_side_effects=True, vmem_limit_bytes=48 * 1024 * 1024
        ),
        name="step",
    )(
        lengths, tokens, cotangent, weight, moment_one, moment_two, hidden, queries, new_keys,
        key_cache, value_cache,
    )
    return finish(queries.shape, *held)


def solution(mesh):
    in_specs = (
        P(("group", "fsdp"), None),
        P(("group", "fsdp"), "tensor"),
        P("fsdp", "tensor"),
        P("fsdp", "tensor"),
        P("fsdp", "tensor"),
        P(None, "group", ("fsdp", "tensor")),
        P(None, ("group", "fsdp", "tensor"), None),
        P(None, ("group", "fsdp", "tensor"), None),
        P(("group", "fsdp", "tensor"), None, None),
        P(("group", "fsdp", "tensor"), None, None),
        P(("group", "fsdp", "tensor")),
    )
    out_specs = (
        P("fsdp", "tensor"),
        P("fsdp", "tensor"),
        P("fsdp", "tensor"),
        P(None, ("group", "fsdp", "tensor"), None),
    )
    sizes = (mesh.shape["group"], mesh.shape["fsdp"], mesh.shape["tensor"])
    return jax.shard_map(
        functools.partial(per_device, *sizes),
        mesh=mesh, in_specs=in_specs, out_specs=out_specs, check_vma=False,
    )
```

```python
import functools

import jax
import jax.numpy as jnp
from jax import lax
from jax.experimental import pallas as pl
from jax.experimental.pallas import tpu as pltpu
from jax.sharding import PartitionSpec as P

HEAD_DIM = 128
GROUP_HEADS = 8
KV_HEADS = 4
STEPS = 4
ADAM_STEP = 10

CHUNKS = 16
PIECES = 2
IN_LAG = 1
MID_LAG = 2
OUT_LAG = 4
ATT_PARTS = 8
MID_ATT_SLOTS = (0, 0, 0, 0, 2, 3, 4, 5)
END_ATT_SLOTS = (1, 1, 2, 3, 4, 5, 7, 9)
AHEAD = 4
EARLY_WAIT = 5

learn_rate = 0.001
beta_one = 0.9
beta_two = 0.95
epsilon = 1e-08
decay_rate = 0.1
masked_score = -1e30

MESH = pl.DeviceIdType.MESH


def adamw(gradient, weight, moment_one, moment_two):
    first_new = beta_one * moment_one + (1.0 - beta_one) * gradient
    second_new = beta_two * moment_two + (1.0 - beta_two) * gradient * gradient
    first_hat = first_new * (1.0 / (1.0 - beta_one**ADAM_STEP))
    second_hat = second_new * (1.0 / (1.0 - beta_two**ADAM_STEP))
    stepped = weight.astype(jnp.float32) * (
        1.0 - learn_rate * decay_rate
    ) - learn_rate * first_hat / (jnp.sqrt(second_hat) + epsilon)
    return stepped.astype(jnp.bfloat16), first_new, second_new


def kernel(
    n_g, n_f, n_t, n_c, early,
    lens, tokens, cot, weight, mom1, mom2, hidden, queries, new_keys, kcache, vcache,
    w_v, m1_v, m2_v, oc, pf, fresh,
    tok, cots, hid, own, sb, r1, r2, gt, other, q_v, nk_v, kc_v, vc_v,
    acc, ps, pr,
    tok_s, tok_r, cot_s, cot_r, hid_s, hid_r, in_s, out_s, r1_r, back_r, other_s, other_r,
    pr_s, pr_r, loc,
):
    g = lax.axis_index("group")
    f = lax.axis_index("fsdp")
    t = lax.axis_index("tensor")
    n_ft = n_f * n_t
    me = f * n_t + t
    rows_c = tok.shape[3]
    rows = n_c * rows_c
    per_t = n_c // n_t
    n_z = n_c + early
    row_dev = kc_v.shape[0]
    cache = kc_v.shape[1]
    width = cot.shape[1]

    mid_l, mid_r = n_g // 2 - 1, n_g // 2
    on_left = g <= mid_l
    toward = jnp.where(on_left, 1, -1)
    depth = jnp.where(on_left, g, n_g - 1 - g)
    mid_depth = jnp.where(on_left, mid_l, n_g - 1 - mid_r)
    is_mid = depth == mid_depth
    max_depth = max(mid_l, n_g - 1 - mid_r)

    barrier = pltpu.get_barrier_semaphore()
    for k in range(1, n_ft):
        peer = lax.rem(me + k, n_ft)
        pl.semaphore_signal(
            barrier, inc=1, device_id={"fsdp": peer // n_t, "tensor": peer % n_t}, device_id_type=MESH
        )

    def tell(to):
        pl.semaphore_signal(
            barrier, inc=1, device_id={"group": lax.rem(g + to + n_g, n_g)}, device_id_type=MESH
        )

    @pl.when(is_mid)
    def _():
        tell(toward)

    def local(src, dst, sem):
        copy = pltpu.make_async_copy(src, dst, sem)
        copy.start()
        return copy

    def row_block(c):
        return lax.rem(jnp.maximum(c - early, 0) + t * per_t, n_c)

    def across(i):
        return (i // 2 * 2 + 2) % n_f + i % 2

    def tok_column(c, to):
        owner = jnp.where(c == 1, across(to), to) if early else to
        return pl.multiple_of(owner * rows + row_block(c) * rows_c, rows_c)

    def tok_local(c):
        return pltpu.make_async_copy(
            tokens.at[:, pl.ds(tok_column(c, f), rows_c)], tok.at[c, 0], tok_r.at[c]
        )

    def hid_local(j):
        return pltpu.make_async_copy(
            hidden.at[:, :, pl.ds(j * rows_c, rows_c)], hid.at[t * per_t + j], hid_r.at[t * per_t + j]
        )

    cot_l = local(cot, cots.at[0], loc.at[0])
    loads_att = [
        local(queries, q_v, loc.at[1]),
        local(new_keys, nk_v, loc.at[2]),
        local(kcache, kc_v, loc.at[3]),
        local(vcache, vc_v, loc.at[4]),
    ]
    for c in range(AHEAD):
        tok_local(c).start()

    @pl.when((depth == 0) & jnp.logical_not(is_mid))
    def _():
        pl.semaphore_wait(barrier, n_ft - 1)

    @pl.when((depth == 0) & is_mid)
    def _():
        pl.semaphore_wait(barrier, n_ft)

    @pl.when((depth > 0) & jnp.logical_not(is_mid))
    def _():
        pl.semaphore_wait(barrier, n_ft)
        tell(-toward)

    @pl.when((depth > 0) & is_mid)
    def _():
        pl.semaphore_wait(barrier, n_ft + 1)
        tell(-toward)

    @pl.when(jnp.logical_not(is_mid))
    def _():
        tell(toward)

    def fsdp_peer(k):
        return (f // 2 * 2 + k // 2 * 2) % n_f + (f % 2 + k % 2) % 2

    def cot_copy(k):
        return pltpu.make_async_remote_copy(
            src_ref=cots.at[k - 1] if k % 2 and k > 1 else cot, dst_ref=cots.at[k],
            send_sem=cot_s.at[0], recv_sem=cot_r.at[k],
            device_id={"fsdp": fsdp_peer(1 if k % 2 else k)}, device_id_type=MESH,
        )

    def tok_copy(c, k):
        peer = fsdp_peer(k)
        return pltpu.make_async_remote_copy(
            src_ref=tokens.at[:, pl.ds(tok_column(c, peer), rows_c)], dst_ref=tok.at[c, k],
            send_sem=tok_s.at[min(k, 2) - 1], recv_sem=tok_r.at[c],
            device_id={"fsdp": peer}, device_id_type=MESH,
        )

    def hid_copy(j, k):
        return pltpu.make_async_remote_copy(
            src_ref=hidden.at[:, :, pl.ds(j * rows_c, rows_c)], dst_ref=hid.at[t * per_t + j],
            send_sem=hid_s.at[0], recv_sem=hid_r.at[t * per_t + j],
            device_id={"tensor": lax.rem(t + k, n_t)}, device_id_type=MESH,
        )

    def arrived(ref, sem):
        pltpu.make_async_copy(ref, ref, sem).wait()

    def send_tokens(c):
        @pl.when((early == 0) | (c >= 2))
        def _():
            for k in range(n_f - 1, 1, -1):
                tok_copy(c, k).start()

        tok_copy(c, 1).start()

    for k in range(2, n_f, 2):
        cot_copy(k).start()
    cot_copy(1).start()
    for c in range(AHEAD):
        send_tokens(c)

    loads_adam = [
        local(weight, w_v, loc.at[5]),
        local(mom1, m1_v, loc.at[6]),
        local(mom2, m2_v, loc.at[7]),
    ]
    for copy in loads_att:
        copy.wait()

    heads_part = KV_HEADS * GROUP_HEADS // ATT_PARTS

    def attend(part):
        h = part * heads_part // GROUP_HEADS
        qs = [
            q_v[:, :, pl.ds(pl.multiple_of((part * heads_part + j) * HEAD_DIM, HEAD_DIM), HEAD_DIM)]
            .reshape(STEPS * row_dev, HEAD_DIM)
            for j in range(heads_part)
        ]
        q = jnp.concatenate(qs, axis=0)
        cols = pl.ds(pl.multiple_of(h * HEAD_DIM, HEAD_DIM), HEAD_DIM)
        kk = kc_v[:, :, cols].reshape(row_dev * cache, HEAD_DIM)
        fk = nk_v[:, :, cols].reshape(STEPS * row_dev, HEAD_DIM)
        vv = vc_v[:, :, cols].reshape(row_dev * cache, HEAD_DIM)
        contract = (((1,), (1,)), ((), ()))
        scale = HEAD_DIM ** (-0.5)
        s_c = lax.dot_general(q, kk, contract, preferred_element_type=jnp.float32) * scale
        s_f = lax.dot_general(q, fk, contract, preferred_element_type=jnp.float32) * scale
        n_q = q.shape[0]
        col_c = lax.broadcasted_iota(jnp.int32, (1, row_dev * cache), 1)
        col_row = col_c // cache
        limit = jnp.zeros_like(col_c)
        for r in range(row_dev):
            limit = jnp.where(col_row == r, lens[r], limit)
        col_row = jnp.where(col_c % cache < limit, col_row, -1)
        q_id = lax.broadcasted_iota(jnp.int32, (n_q, 1), 0)
        q_row = q_id % row_dev
        q_step = (q_id // row_dev) % STEPS
        col_f = lax.broadcasted_iota(jnp.int32, (1, STEPS * row_dev), 1)
        ok_c = q_row == col_row
        ok_f = (q_row == col_f % row_dev) & (col_f // row_dev <= q_step)
        s_c = jnp.where(ok_c, s_c, masked_score)
        s_f = jnp.where(ok_f, s_f, masked_score)
        highest = jnp.maximum(
            jnp.max(s_c, axis=-1, keepdims=True), jnp.max(s_f, axis=-1, keepdims=True)
        )
        e_c = jnp.exp(s_c - highest)
        e_f = jnp.exp(s_f - highest)
        den = jnp.sum(e_c, axis=-1, keepdims=True) + jnp.sum(e_f, axis=-1, keepdims=True)
        p_c = (e_c / den).astype(jnp.bfloat16)
        pf[part] = (e_f / den).astype(jnp.bfloat16)
        oc[part] = jnp.dot(p_c, vv, preferred_element_type=jnp.float32)

    acc[...] = jnp.zeros_like(acc)
    cot_l.wait()
    cot_copy(1).wait_recv()

    def cot_rest():
        for k in range(2, n_f, 2):
            cot_copy(k).wait_recv()
            cot_copy(k + 1).start()

    def cot_ready():
        for k in range(3, n_f, 2):
            cot_copy(k).wait_recv()

    if not early:
        cot_rest()
        cot_ready()

    @pl.when(jnp.logical_not(is_mid))
    def _():
        pl.semaphore_wait(barrier, 1)

    def parts_done(s):
        mid = sum((s >= at).astype(jnp.int32) for at in MID_ATT_SLOTS)
        end = sum((s >= at).astype(jnp.int32) for at in END_ATT_SLOTS)
        return jnp.where(is_mid, mid, end)

    window = r1_r.shape[0]

    def inward(c, p, dst, recv):
        return pltpu.make_async_remote_copy(
            src_ref=sb.at[c, p], dst_ref=dst.at[c, p], send_sem=in_s.at[0], recv_sem=recv.at[lax.rem(c, window), p],
            device_id={"group": lax.rem(g + toward + n_g, n_g)}, device_id_type=MESH,
        )

    def outward(c, p):
        return pltpu.make_async_remote_copy(
            src_ref=gt.at[c, p], dst_ref=gt.at[c, p], send_sem=out_s.at[0], recv_sem=back_r.at[lax.rem(c, window), p],
            device_id={"group": lax.rem(g - toward + n_g, n_g)}, device_id_type=MESH,
        )

    def send_inward(c, p, part):
        sb[c, p] = part.astype(jnp.bfloat16)

        @pl.when(is_mid)
        def _():
            inward(c, p, r2, back_r).start()

        @pl.when(jnp.logical_not(is_mid))
        def _():
            inward(c, p, r1, r1_r).start()

    def active(c):
        return (c >= 0) & (c < n_z)

    def to_other():
        return pltpu.make_async_remote_copy(
            src_ref=gt.at[1], dst_ref=other, send_sem=other_s.at[0], recv_sem=other_r.at[0],
            device_id={"fsdp": fsdp_peer(2)}, device_id_type=MESH,
        )

    pieces, piece = sb.shape[1:3]
    first_total = IN_LAG * max_depth + MID_LAG

    def gradient(block, cot_block):
        k = block.shape[0] * block.shape[1]
        return lax.dot_general(
            block.reshape(k, rows_c), cot_block.reshape(k, width), (((0,), (0,)), ((), ())),
            preferred_element_type=jnp.float32,
        )

    def place(s, grad):
        @pl.when(depth == 0)
        def _():
            for p in range(pieces):
                send_inward(s, p, grad[p * piece : (p + 1) * piece])

        @pl.when(depth > 0)
        def _():
            for p in range(pieces):
                own[s, p] = grad[p * piece : (p + 1) * piece]

    def update(b, grad):
        arrived(hid.at[b], hid_r.at[b])
        span = pl.ds(pl.multiple_of(b * rows_c, rows_c), rows_c)
        w_new, m1_new, m2_new = adamw(
            grad.reshape(rows_c, width), w_v[span], m1_v[span], m2_v[span]
        )
        w_v[span] = w_new
        m1_v[span] = m1_new
        m2_v[span] = m2_new
        lhs = hid[b].reshape(acc.shape[0], rows_c)
        acc[...] += jnp.dot(lhs, w_new, preferred_element_type=jnp.float32)

    last_total = first_total + OUT_LAG * max_depth
    to_other_at = max(n_z - 1, last_total + 2)
    early_at = to_other_at + EARLY_WAIT

    def slot(s, carry):
        @pl.when(s < n_z - AHEAD)
        def _():
            tok_local(s + AHEAD).start()
            send_tokens(s + AHEAD)

        @pl.when(s < per_t)
        def _():
            for k in range(1, n_t):
                hid_copy(s, k).start()
            hid_local(s).start()

        if early:

            @pl.when(s < 2)
            def _():
                arrived(tok.at[s, pl.ds(0, 2)], tok_r.at[s])
                place(s, gradient(tok[s, 0:2], cots[0:2]))

            @pl.when(s == 2)
            def _():
                cot_ready()

        @pl.when((s >= 2 * early) & (s < n_z))
        def _():
            arrived(tok.at[s], tok_r.at[s])
            place(s, gradient(tok[s], cots[...]))

        c1 = s - IN_LAG * depth

        @pl.when((depth > 0) & active(c1))
        def _():
            for p in range(pieces):
                inward(c1, p, r1, r1_r).wait_recv()
                send_inward(c1, p, own[c1, p] + r1[c1, p].astype(jnp.float32))

        @pl.when(s == first_total)
        def _():
            for copy in loads_adam:
                copy.wait()

        c2 = s - first_total - OUT_LAG * (mid_depth - depth)
        c3 = c2 - 1

        @pl.when((c3 >= 2 * early) & (c3 < n_z))
        def _():
            update(row_block(c3), gt[c3].astype(jnp.float32))

        if early:

            @pl.when(s == to_other_at)
            def _():
                to_other().start()

            @pl.when(s == early_at)
            def _():
                to_other().wait_recv()
                update(row_block(0), gt[0].astype(jnp.float32) + other[...].astype(jnp.float32))

        def attend_next(part, none):
            attend(part)
            return none

        lax.fori_loop(parts_done(s - 1), parts_done(s), attend_next, 0)

        if early:

            @pl.when(s == 1)
            def _():
                cot_rest()

        @pl.when(active(c2))
        def _():
            @pl.when(is_mid)
            def _():
                for p in range(pieces):
                    inward(c2, p, r2, back_r).wait_recv()
                    total = sb[c2, p].astype(jnp.float32) + r2[c2, p].astype(jnp.float32)
                    gt[c2, p] = total.astype(jnp.bfloat16)

                    @pl.when(depth > 0)
                    def _():
                        outward(c2, p).start()

            @pl.when(jnp.logical_not(is_mid))
            def _():
                for p in range(pieces):
                    outward(c2, p).wait_recv()

                    @pl.when(depth > 0)
                    def _():
                        outward(c2, p).start()

        return carry

    slots = max(n_z + last_total + 1, max(MID_ATT_SLOTS + END_ATT_SLOTS) + 1, early_at + 1 if early else 0)
    lax.fori_loop(0, slots, slot, 0)

    def out_copy(k):
        peer = lax.rem(me + k, n_ft)
        return pltpu.make_async_remote_copy(
            src_ref=ps.at[k], dst_ref=pr.at[t * n_f + f], send_sem=pr_s.at[0], recv_sem=pr_r.at[0],
            device_id={"fsdp": peer // n_t, "tensor": peer % n_t}, device_id_type=MESH,
        )

    ps_all = acc.reshape(STEPS, acc.shape[0] // STEPS, width)
    for k in range(1, n_ft):
        peer = lax.rem(me + k, n_ft)
        take = pl.ds(pl.multiple_of(peer * row_dev, row_dev), row_dev)
        ps[k] = ps_all[:, take, :].reshape(STEPS * row_dev, width).astype(jnp.bfloat16)
        out_copy(k).start()
    take = pl.ds(pl.multiple_of(me * row_dev, row_dev), row_dev)
    pr[t * n_f + f] = ps_all[:, take, :].reshape(STEPS * row_dev, width).astype(jnp.bfloat16)
    arrived(cots.at[pl.ds(1, n_f - 1)], cot_s.at[0])
    arrived(tok.at[:, pl.ds(0, 1)], tok_s.at[0])
    arrived(tok.at[pl.ds(2 * early, n_z - 2 * early), pl.ds(2, n_f - 2)], tok_s.at[1])
    if early:
        to_other().wait_send()
    arrived(hid.at[pl.ds(0, per_t * (n_t - 1))], hid_s.at[0])
    arrived(sb, in_s.at[0])

    @pl.when(depth > 0)
    def _():
        arrived(gt, out_s.at[0])

    arrived(pr.at[pl.ds(0, n_ft - 1)], pr_r.at[0])
    fresh_parts = []
    for tt in range(n_t):
        total = pr[tt * n_f].astype(jnp.float32)
        for ff in range(1, n_f):
            total = total + pr[tt * n_f + ff].astype(jnp.float32)
        fresh_parts.append(total.astype(jnp.bfloat16))
    fresh[...] = jnp.concatenate(fresh_parts, axis=1)

    arrived(ps.at[pl.ds(0, n_ft - 1)], pr_s.at[0])


def finish_kernel(w_v, m1_v, m2_v, oc, pf, fresh, w_o, m1_o, m2_o, att_o, att_v, sems):
    copies = []
    for a, o, cuts in ((m1_v, m1_o, 4), (m2_v, m2_o, 4), (w_v, w_o, 2)):
        rows = a.shape[0] // cuts
        for j in range(cuts):
            span = pl.ds(j * rows, rows)
            copies.append(pltpu.make_async_copy(a.at[span], o.at[span], sems.at[len(copies)]))
            copies[-1].start()
    heads_part = KV_HEADS * GROUP_HEADS // ATT_PARTS
    steps, row_dev = att_v.shape[:2]
    block = steps * row_dev
    for part in range(ATT_PARTS):
        h = part * heads_part // GROUP_HEADS
        res = oc[part] + jnp.dot(
            pf[part], fresh[:, h * HEAD_DIM : (h + 1) * HEAD_DIM], preferred_element_type=jnp.float32
        )
        for j in range(heads_part):
            at = (part * heads_part + j) * HEAD_DIM
            att_v[:, :, at : at + HEAD_DIM] = (
                res[j * block : (j + 1) * block].reshape(steps, row_dev, HEAD_DIM).astype(jnp.bfloat16)
            )
        cols = pl.ds(part * heads_part * HEAD_DIM, heads_part * HEAD_DIM)
        copies.append(
            pltpu.make_async_copy(att_v.at[:, :, cols], att_o.at[:, :, cols], sems.at[len(copies)])
        )
        copies[-1].start()
    for copy in copies:
        copy.wait()


def finish(att_shape, w, m1, m2, *rest):
    spec = pl.BlockSpec(memory_space=pl.ANY)
    outs = [jax.ShapeDtypeStruct(a.shape, a.dtype) for a in (w, m1, m2)]
    outs.append(jax.ShapeDtypeStruct(att_shape, jnp.bfloat16))
    held = [pltpu.with_memory_space_constraint(a, pltpu.VMEM) for a in (w, m1, m2) + rest]
    return pl.pallas_call(
        finish_kernel,
        out_shape=tuple(outs),
        in_specs=[pl.BlockSpec(memory_space=pltpu.VMEM)] * len(held),
        out_specs=(spec,) * 4,
        scratch_shapes=[pltpu.VMEM(att_shape, jnp.bfloat16), pltpu.SemaphoreType.DMA((10 + ATT_PARTS,))],
        compiler_params=pltpu.CompilerParams(vmem_limit_bytes=16 * 1024 * 1024),
        name="finish",
    )(*held)


def per_device(
    n_g, n_f, n_t,
    tokens, cotangent, weight, moment_one, moment_two, hidden, queries, new_keys,
    key_cache, value_cache, lengths,
):
    n_ft = n_f * n_t
    rows, width = weight.shape
    n_c = max(CHUNKS, n_t)
    rows_c = rows // n_c
    row_dev, cache, kvw = key_cache.shape
    tok_rows = tokens.shape[0]
    early = 1 if n_f == 4 else 0
    n_z = n_c + early
    max_depth = max(n_g // 2 - 1, n_g - 1 - n_g // 2)
    window = min(n_z, IN_LAG * max_depth + MID_LAG + OUT_LAG * max_depth + 2)
    piece_shape = (n_z, PIECES, rows_c // PIECES, width)
    acc_rows = hidden.shape[0] * hidden.shape[1]
    n_q = KV_HEADS * GROUP_HEADS // ATT_PARTS * STEPS * row_dev
    bf16, f32 = jnp.bfloat16, jnp.float32
    dma = pltpu.SemaphoreType.DMA
    anywhere = pl.BlockSpec(memory_space=pl.ANY)
    scratch = [
        pltpu.VMEM((n_z, n_f, tok_rows, rows_c), bf16),
        pltpu.VMEM((n_f, tok_rows, width), bf16),
        pltpu.VMEM((n_c,) + hidden.shape[:2] + (rows_c,), bf16),
        pltpu.VMEM(piece_shape, f32),
        pltpu.VMEM(piece_shape, bf16),
        pltpu.VMEM(piece_shape, bf16),
        pltpu.VMEM(piece_shape, bf16),
        pltpu.VMEM(piece_shape, bf16),
        pltpu.VMEM(piece_shape[1:], bf16),
        pltpu.VMEM(queries.shape, bf16),
        pltpu.VMEM(new_keys.shape, bf16),
        pltpu.VMEM(key_cache.shape, bf16),
        pltpu.VMEM(value_cache.shape, bf16),
        pltpu.VMEM((acc_rows, width), f32),
        pltpu.VMEM((n_ft, STEPS * row_dev, width), bf16),
        pltpu.VMEM((n_ft, STEPS * row_dev, width), bf16),
        dma((2,)), dma((n_z,)),
        dma((1,)), dma((n_f,)),
        dma((1,)), dma((n_c,)),
        dma((1,)), dma((1,)), dma((window, PIECES)), dma((window, PIECES)), dma((1,)), dma((1,)),
        dma((1,)), dma((1,)), dma((8,)),
    ]
    held = pl.pallas_call(
        functools.partial(kernel, n_g, n_f, n_t, n_c, early),
        out_shape=(
            pltpu.VMEM(weight.shape, bf16),
            pltpu.VMEM(weight.shape, f32),
            pltpu.VMEM(weight.shape, f32),
            pltpu.VMEM((ATT_PARTS, n_q, HEAD_DIM), f32),
            pltpu.VMEM((ATT_PARTS, n_q, STEPS * row_dev), bf16),
            pltpu.VMEM((STEPS * row_dev, n_t * width), bf16),
        ),
        in_specs=[pl.BlockSpec(memory_space=pltpu.SMEM)] + [anywhere] * 10,
        out_specs=(pl.BlockSpec(memory_space=pltpu.VMEM),) * 6,
        scratch_shapes=scratch,
        compiler_params=pltpu.CompilerParams(
            collective_id=0, has_side_effects=True, vmem_limit_bytes=48 * 1024 * 1024
        ),
        name="step",
    )(
        lengths, tokens, cotangent, weight, moment_one, moment_two, hidden, queries, new_keys,
        key_cache, value_cache,
    )
    return finish(queries.shape, *held)


def solution(mesh):
    in_specs = (
        P(("group", "fsdp"), None),
        P(("group", "fsdp"), "tensor"),
        P("fsdp", "tensor"),
        P("fsdp", "tensor"),
        P("fsdp", "tensor"),
        P(None, "group", ("fsdp", "tensor")),
        P(None, ("group", "fsdp", "tensor"), None),
        P(None, ("group", "fsdp", "tensor"), None),
        P(("group", "fsdp", "tensor"), None, None),
        P(("group", "fsdp", "tensor"), None, None),
        P(("group", "fsdp", "tensor")),
    )
    out_specs = (
        P("fsdp", "tensor"),
        P("fsdp", "tensor"),
        P("fsdp", "tensor"),
        P(None, ("group", "fsdp", "tensor"), None),
    )
    sizes = (mesh.shape["group"], mesh.shape["fsdp"], mesh.shape["tensor"])
    return jax.shard_map(
        functools.partial(per_device, *sizes),
        mesh=mesh, in_specs=in_specs, out_specs=out_specs, check_vma=False,
    )
```
